1024 devices in a mesh: wide: 64 (over y_hi, x, core), narrow: 16 (over y_lo, z).
Axes of the slice: x: 8, y: 8 (y_hi: 4, y_lo: 2; y = y_hi * 2 + y_lo), z: 8, core: 2. Of those that a mesh axis runs over, the one named last changes fastest.
Arguments:
- amplitude: float32 [65536, 256], P(('wide', 'narrow')), may hold values from -6 to 6
- tilt: float32 [3, 65536], P(None, ('wide', 'narrow')), may hold values from -3.140625 to 3.140625
- owner: int32 [65536, 1], P(('wide', 'narrow')), may hold values from 0 to 63; in each aligned block of 64 rows (0 to 63, 64 to 127, ...) at most 3 rows name the same one
- row_offset: int32 [65536], P(('wide', 'narrow')), may hold values from 0 to 496
- col_offset: int32 [65536], P(('wide', 'narrow')), may hold values from 0 to 240
Outputs:
- hologram: float32 [2, 8192, 16384], P(None, 'narrow', 'wide')
The draws below stay inside these ranges and needn't reach their ends.
Inputs may be any that keep to these rules, and one draw needn't show every extreme that they name: `owner`: among the 64 facets of one device no tile column is named more than 3 times, and on some device one column is named exactly 3 times.
All inputs are finite; a program needn't handle non-finite values.
Results may differ from the reference program's by a relative error of at most 0.0085.
Values may be sent and summed in bfloat16 or wider, within the bound.
No kernel may reach another device: no remote copies, remote signals or barrier semaphores. Data moves between devices by JAX's collectives and lax.ppermute only.
A program may use at most 32 MiB of HBM per device.

```python
import math
import jax
import jax.numpy as jnp
import numpy as np
from jax import lax

TH = 512
TW = 256
FACET = 16
FAC_DEV = 64
CAP = 3
DEPTH = 1280
FACETS = 65536
NY = 8192
NX = 16384
N_WIDE = 64
N_NARROW = 16


def with_ends(array, stream_key, low, top_value):
    longest = array.shape.index(max(array.shape))
    spots = []
    for shift in (0, 1):
        where = [jax.random.randint(jax.random.fold_in(stream_key, axis), (), 0, length) for axis, length in enumerate(array.shape)]
        where[longest] = (where[longest] + shift) % array.shape[longest]
        spots.append(tuple(where))
    return array.at[spots[0]].set(low).at[spots[1]].set(top_value)


def block_levels(key, extent, split, low, top_value):
    factor_of = 1.0
    for axis_at, blocks in split:
        steps = jax.random.uniform(jax.random.fold_in(jax.random.fold_in(key, 6), axis_at), (blocks,), jnp.float32, low / len(split), top_value / len(split))
        factor_of = factor_of * jnp.repeat(jnp.exp(steps), extent[axis_at] // blocks).reshape((-1,) + (1,) * (len(extent) - 1 - axis_at))
    return factor_of


def deal_out(key, own, number, rows, count, top, bound, slope):
    sequence = jax.random.permutation(key, count)
    packed, ordinary = portions_of(count, rows * top, bound, slope, True), portions_of(count, rows * top, bound, slope, False)
    places = jnp.arange(count)

    def named(lengths, turn):
        used = int((lengths > 0).sum())
        fixed = max(1, used // 4)
        moved = fixed + (places - fixed + turn * (used - fixed)) % max(1, count - fixed)
        return jnp.zeros((count,), jnp.int32).at[sequence[jnp.where(places < fixed, places, moved)]].set(jnp.asarray(lengths, jnp.int32))

    lengths = jnp.where(number % 4 == 0, named(packed, number // 4), named(ordinary, number - number // 4 - 1))
    mixed = jax.random.permutation(jax.random.fold_in(own, 3), count)
    source_of, receiver = mixed[0:count // 2 * 2:2], mixed[1:count // 2 * 2:2]
    margin = jnp.minimum(lengths[source_of] - 1, bound - lengths[receiver]) // 2
    margin = jnp.where((source_of == sequence[0]) | (receiver == sequence[0]) | (lengths[receiver] == 0), 0, jnp.maximum(margin, 0))
    moved = jax.random.randint(jax.random.fold_in(own, 4), (count // 2,), 0, 1 << 20) % (margin + 1)
    lengths = lengths.at[source_of].add(-moved).at[receiver].add(moved)
    labels = jnp.searchsorted(jnp.cumsum(lengths), jnp.arange(rows * top), side="right").astype(jnp.int32)
    table = labels.reshape(top, rows).T
    table = table[jax.random.permutation(jax.random.fold_in(own, 1), rows)]
    turn = jax.random.randint(jax.random.fold_in(own, 2), (rows, 1), 0, top)
    return jnp.take_along_axis(table, (jnp.arange(top)[None, :] + turn) % top, axis=1)


def portions_of(count, total, limit, slope, full):
    weights = [(1 << 20) // math.isqrt(standing ** slope) + 1 for standing in range(1, count + 1)]
    largest = limit if full else min(limit, max(-(-total // count), total * weights[0] // sum(weights)))
    least = 1 if total - largest >= count - 1 else 0
    given, rest = [largest] + [least] * (count - 1), total - largest - least * (count - 1)
    while rest > 0:
        candidates = [i for i in range(1, count) if given[i] < largest] or [i for i in range(1, count) if given[i] < limit]
        whole, left = sum([weights[i] for i in candidates]), rest
        for i in candidates:
            more = min(limit - given[i], max(1, left * weights[i] // whole), rest)
            given[i] = given[i] + more
            rest = rest - more
    return np.array(given)


def bell_draw(stream_key, shape, width, limit, cuts=(), held_as=jnp.bfloat16):
    entries = width * jax.random.normal(stream_key, shape, jnp.float32)
    if cuts:
        entries = entries * block_levels(stream_key, shape, cuts, -0.22, 0.18)
    return jnp.clip(entries, -limit, limit).astype(held_as)


def setup_inputs(seed: int = 0) -> dict:
    keys = jax.random.split(jax.random.key(seed), 6)
    amplitude = bell_draw(keys[0], (FACETS, FACET * FACET), 1.0, 6.0, ((0, 1024),), jnp.float32)
    tilt = jnp.clip(jax.random.uniform(keys[1], (3, FACETS), jnp.float32, -3.140625, 3.140625), -3.140625, 3.140625)
    owner_keys = jax.random.split(jax.random.fold_in(keys[2], 1), FACETS // FAC_DEV)
    owner_turns = jax.random.permutation(jax.random.fold_in(keys[2], 3), FACETS // FAC_DEV)
    owner = jax.vmap(lambda own, number: deal_out(jax.random.fold_in(keys[2], 2), own, number, FAC_DEV, N_WIDE, 1, CAP, 2))(owner_keys, owner_turns).reshape((FACETS, 1))
    row_offset = with_ends(jax.random.randint(keys[3], (FACETS,), 0, TH - FACET + 1), jax.random.fold_in(keys[3], 1), 0, TH - FACET).astype(jnp.int32)
    col_offset = with_ends(jax.random.randint(keys[4], (FACETS,), 0, TW - FACET + 1), jax.random.fold_in(keys[4], 1), 0, TW - FACET).astype(jnp.int32)
    return dict(amplitude=amplitude, tilt=tilt, owner=owner, row_offset=row_offset, col_offset=col_offset)


reach_spread = 16.0

def dft_tables(length, spin_sign):
    position = jnp.arange(length, dtype=jnp.int32)
    product = position[:, None] * position[None, :] % length
    angles = product.astype(jnp.float32) * (2.0 * math.pi / length)
    return (jnp.cos(angles).astype(jnp.bfloat16), (spin_sign * jnp.sin(angles)).astype(jnp.bfloat16))

def signed_frequency(length):
    position = jnp.arange(length, dtype=jnp.int32)
    return (position + length // 2) % length - length // 2

def reach_weight(length, depth_cells, offset):
    travel = signed_frequency(length).astype(jnp.float32) * (depth_cells / (length * length))
    return jnp.exp(-(travel - offset) ** 2 / reach_spread)

def depth_phase(length, depth_cells):
    frequency = signed_frequency(length)
    turn_count = depth_cells * frequency * frequency % (2 * length * length)
    return turn_count.astype(jnp.float32) * (-math.pi / (length * length))

def render(amplitude, tilt, patch):
    position = jnp.arange(patch * patch, dtype=jnp.int32)
    row_pos = (position // patch).astype(jnp.float32)
    col_pos = (position % patch).astype(jnp.float32)
    phase = tilt[0][:, None] * row_pos[None, :] + tilt[1][:, None] * col_pos[None, :] + tilt[2][:, None]
    return ((amplitude * jnp.cos(phase)).astype(jnp.bfloat16), (amplitude * jnp.sin(phase)).astype(jnp.bfloat16))

def left_apply(table_r, table_i, real_part, imag_part):
    real_real = jnp.dot(table_r, real_part, preferred_element_type=jnp.float32)
    imag_imag = jnp.dot(table_i, imag_part, preferred_element_type=jnp.float32)
    real_imag = jnp.dot(table_r, imag_part, preferred_element_type=jnp.float32)
    imag_real = jnp.dot(table_i, real_part, preferred_element_type=jnp.float32)
    return (real_real - imag_imag, real_imag + imag_real)

def tile_right(real_part, imag_part, table_r, table_i):
    real_wide = real_part.astype(jnp.float32)
    imag_wide = imag_part.astype(jnp.float32)
    tab_r = table_r.astype(jnp.float32)
    tab_i = table_i.astype(jnp.float32)
    high = lax.Precision.HIGHEST
    real_real = jnp.einsum('ywk,kx->ywx', real_wide, tab_r, precision=high)
    imag_imag = jnp.einsum('ywk,kx->ywx', imag_wide, tab_i, precision=high)
    real_imag = jnp.einsum('ywk,kx->ywx', real_wide, tab_i, precision=high)
    imag_real = jnp.einsum('ywk,kx->ywx', imag_wide, tab_r, precision=high)
    return (real_real - imag_imag, real_imag + imag_real)

def reference(amplitude, tilt, owner, row_offset, col_offset):
    field_r, field_i = render(amplitude, tilt, FACET)
    position = jnp.arange(FACET * FACET, dtype=jnp.int32)
    band = jnp.arange(FACETS, dtype=jnp.int32) // FAC_DEV % N_NARROW
    rows_at = (band * TH + row_offset)[:, None] + (position // FACET)[None, :]
    cols_at = (owner[:, 0] * TW + col_offset)[:, None] + (position % FACET)[None, :]
    plane_r = jnp.zeros((NY, NX), jnp.float32).at[rows_at, cols_at].add(field_r.astype(jnp.float32)).astype(jnp.bfloat16)
    plane_i = jnp.zeros((NY, NX), jnp.float32).at[rows_at, cols_at].add(field_i.astype(jnp.float32)).astype(jnp.bfloat16)
    fwd_hr, fwd_hi = dft_tables(TH, -1.0)
    fwd_wr, fwd_wi = dft_tables(TW, -1.0)
    inv_hr, inv_hi = dft_tables(TH, 1.0)
    inv_wr, inv_wi = dft_tables(TW, 1.0)
    scale = 1.0 / math.sqrt(TH * TW)

    def forward_band(pair):
        band_r, band_i = pair
        rows_r, rows_i = left_apply(fwd_hr, fwd_hi, band_r, band_i)
        rows_r = rows_r.astype(jnp.bfloat16).reshape(TH, N_WIDE, TW)
        rows_i = rows_i.astype(jnp.bfloat16).reshape(TH, N_WIDE, TW)
        spec_r, spec_i = tile_right(rows_r, rows_i, fwd_wr, fwd_wi)
        return ((spec_r * scale).astype(jnp.bfloat16), (spec_i * scale).astype(jnp.bfloat16))
    spec_r, spec_i = lax.map(forward_band, (plane_r.reshape(N_NARROW, TH, NX), plane_i.reshape(N_NARROW, TH, NX)))
    pad_r = jnp.pad(spec_r, ((0, 0), (0, 0), (2, 2), (0, 0)))
    pad_i = jnp.pad(spec_i, ((0, 0), (0, 0), (2, 2), (0, 0)))
    col_r = jnp.zeros(spec_r.shape, jnp.float32)
    col_i = jnp.zeros(spec_i.shape, jnp.float32)
    for offset in range(-2, 3):
        weight = reach_weight(TW, DEPTH, float(offset))
        start = 2 - offset
        col_r = col_r + weight * pad_r[:, :, start:start + N_WIDE, :].astype(jnp.float32)
        col_i = col_i + weight * pad_i[:, :, start:start + N_WIDE, :].astype(jnp.float32)
    col_r = col_r.astype(jnp.bfloat16)
    col_i = col_i.astype(jnp.bfloat16)
    pad_r = jnp.pad(col_r, ((2, 2), (0, 0), (0, 0), (0, 0)))
    pad_i = jnp.pad(col_i, ((2, 2), (0, 0), (0, 0), (0, 0)))
    sum_r = jnp.zeros(col_r.shape, jnp.float32)
    sum_i = jnp.zeros(col_i.shape, jnp.float32)
    for offset in range(-2, 3):
        weight = reach_weight(TH, DEPTH, float(offset))[None, :, None, None]
        start = 2 - offset
        sum_r = sum_r + weight * pad_r[start:start + N_NARROW].astype(jnp.float32)
        sum_i = sum_i + weight * pad_i[start:start + N_NARROW].astype(jnp.float32)
    angle = depth_phase(TH, DEPTH)[:, None] + depth_phase(TW, DEPTH)[None, :]
    phase_r = jnp.cos(angle)[None, :, None, :]
    phase_i = jnp.sin(angle)[None, :, None, :]
    focus_r = (phase_r * sum_r - phase_i * sum_i).astype(jnp.bfloat16)
    focus_i = (phase_r * sum_i + phase_i * sum_r).astype(jnp.bfloat16)

    def inverse_band(pair):
        band_r, band_i = pair
        cols_r, cols_i = tile_right(band_r, band_i, inv_wr, inv_wi)
        cols_r = cols_r.astype(jnp.bfloat16).reshape(TH, NX)
        cols_i = cols_i.astype(jnp.bfloat16).reshape(TH, NX)
        out_r, out_i = left_apply(inv_hr, inv_hi, cols_r, cols_i)
        return (out_r * scale, out_i * scale)
    holo_r, holo_i = lax.map(inverse_band, (focus_r, focus_i))
    return jnp.stack([holo_r.reshape(NY, NX), holo_i.reshape(NY, NX)])
```

```python
import functools
import math

import jax
import jax.numpy as jnp
from jax import lax
from jax.experimental import pallas as pl
from jax.experimental.pallas import tpu as pltpu
from jax.sharding import PartitionSpec as P

TH = 512
TW = 256
FACET = 16
DEPTH = 1280
REACH = 2
OFFSETS = 2 * REACH + 1
CAP = 3
SLOTS = OFFSETS * CAP
ROWS = 16
SPREAD = 16.0
SCALE = 1.0 / math.sqrt(TH * TW)

F32 = jnp.float32
BF16 = jnp.bfloat16
NN = (((1,), (0,)), ((), ()))
NT = (((1,), (1,)), ((), ()))


def mm(a, b, dims=NN):
    return lax.dot_general(a, b, dims, preferred_element_type=F32)


def iota(shape, dim):
    return lax.broadcasted_iota(jnp.int32, shape, dim)


def cis(angle):
    return jnp.cos(angle), jnp.sin(angle)


def signed_frequency(position, length):
    return ((position + length // 2) & (length - 1)) - length // 2


def depth_phase(position, length):
    frequency = signed_frequency(position, length)
    turns = (DEPTH * frequency * frequency) & (2 * length * length - 1)
    return turns.astype(F32) * (-math.pi / (length * length))


def reach_weight(position, length, offset):
    travel = signed_frequency(position, length).astype(F32) * (DEPTH / (length * length))
    return jnp.exp(-((travel - offset) ** 2) / SPREAD)


def from_behind(value, axis, steps):
    count = lax.axis_size(axis)
    leading, last = (max(0, -steps), min(count, count - steps))
    return lax.ppermute(value, axis, [(source, source + steps) for source in range(leading, last)])


def turn_angle(a, b, length):
    return ((a * b) & (length - 1)).astype(F32) * (2.0 * math.pi / length)


def table_kernel(fblk_ref, grow_ref, hblk_ref, kr_ref, ki_ref):
    fine_r, fine_i = cis(-turn_angle(iota((16, TW), 0), iota((16, TW), 1), TW))
    wide_r, wide_i = cis(-turn_angle(iota((16, TW), 0), iota((16, TW), 1), 16))
    for a in range(16):
        real = (wide_r[a : a + 1] * fine_r - wide_i[a : a + 1] * fine_i).astype(BF16)
        imag = (wide_r[a : a + 1] * fine_i + wide_i[a : a + 1] * fine_r).astype(BF16)
        at = 16 * a
        fblk_ref[at : at + 16, :TW] = real
        fblk_ref[at : at + 16, TW:] = -imag
        fblk_ref[TW + at : TW + at + 16, :TW] = imag
        fblk_ref[TW + at : TW + at + 16, TW:] = real
    wide_r, wide_i = cis(
        turn_angle(iota((16, TW), 0), iota((16, TW), 1), 16) + depth_phase(iota((16, TW), 1), TW)
    )
    for a in range(16):
        real = (wide_r[a : a + 1] * fine_r + wide_i[a : a + 1] * fine_i).astype(BF16)
        imag = (wide_i[a : a + 1] * fine_r - wide_r[a : a + 1] * fine_i).astype(BF16)
        at = 16 * a
        hblk_ref[at : at + 16, :TW] = real
        hblk_ref[at : at + 16, TW:] = -imag
        hblk_ref[TW + at : TW + at + 16, :TW] = imag
        hblk_ref[TW + at : TW + at + 16, TW:] = real
    fine_r, fine_i = cis(-turn_angle(iota((16, TH), 0), iota((16, TH), 1), TH))
    wide_r, wide_i = cis(-turn_angle(iota((32, TH), 0), iota((32, TH), 1), 32))
    for p in range(16):
        real = fine_r[p : p + 1] * wide_r - fine_i[p : p + 1] * wide_i
        imag = fine_r[p : p + 1] * wide_i + fine_i[p : p + 1] * wide_r
        grow_ref[32 * p : 32 * p + 32, :TH] = real.astype(BF16)
        grow_ref[32 * p : 32 * p + 32, TH:] = imag.astype(BF16)
    wide_r, wide_i = cis(
        turn_angle(iota((32, TH), 0), iota((32, TH), 1), 32) + depth_phase(iota((32, TH), 1), TH)
    )
    for q in range(32):
        real = wide_r[q : q + 1] * fine_r + wide_i[q : q + 1] * fine_i
        imag = wide_i[q : q + 1] * fine_r - wide_r[q : q + 1] * fine_i
        kr_ref[16 * q : 16 * q + 16, :] = real.astype(BF16)
        ki_ref[16 * q : 16 * q + 16, :] = imag.astype(BF16)


def make_tables():
    square = jax.ShapeDtypeStruct((TH, TH), BF16)
    return pl.pallas_call(
        table_kernel,
        out_shape=(square, jax.ShapeDtypeStruct((TH, 2 * TH), BF16), square, square, square),
        out_specs=tuple([pl.BlockSpec(memory_space=pltpu.VMEM)] * 5),
        compiler_params=pltpu.CompilerParams(vmem_limit_bytes=24 << 20),
        cost_estimate=pl.CostEstimate(flops=8_000_000, bytes_accessed=3 << 20, transcendentals=200_000),
        name="tables",
    )()


def pack_kernel(amp_ref, tilt_ref, owner_ref, row_ref, col_ref, out_ref):
    count = amp_ref.shape[0]
    total = out_ref.shape[0]
    row, col = row_ref[...], col_ref[...]
    owner = owner_ref[...].astype(F32)
    sub, lane = iota((count, count), 0), iota((count, count), 1)

    def upright(vector):
        picked = jnp.where(sub == lane, vector.astype(F32), 0.0)
        return jnp.sum(picked, axis=1, keepdims=True)

    same = (upright(owner) == owner) & (sub < lane)
    rank = jnp.sum(jnp.where(same, 1.0, 0.0), axis=0, keepdims=True)
    key = CAP * owner + rank
    amp = amp_ref[...]
    turn_v = upright(col & 15).astype(jnp.int32)
    turn_u = upright(row & 15).astype(jnp.int32)
    within = iota(amp.shape, 1) & 15
    for step in (1, 2, 4, 8):
        moved = jnp.where(
            within >= step, pltpu.roll(amp, step, 1), pltpu.roll(amp, 240 + step, 1)
        )
        amp = jnp.where((turn_v & step) != 0, moved, amp)
    for step in (1, 2, 4, 8):
        amp = jnp.where((turn_u & step) != 0, pltpu.roll(amp, 16 * step, 1), amp)
    at = iota((total, count), 0)
    wanted = CAP * (at >> 4) + (at & 15) - CAP * REACH
    wanted = jnp.where((at & 15) == SLOTS, -1, wanted).astype(F32)
    chosen = jnp.where(wanted == key, 1.0, 0.0).astype(BF16)
    placed = mm(chosen, amp.astype(BF16))
    tilt = tilt_ref[...]
    high = tilt.astype(BF16).astype(F32)
    middle = (tilt - high).astype(BF16).astype(F32)
    low = tilt - high - middle
    lines = [part[k : k + 1] for part in (high, middle, low) for k in range(3)]
    lines += [(row >> 4).astype(F32), (row & 15).astype(F32), col.astype(F32)]
    entry = iota((16, count), 0)
    extras = jnp.zeros((16, count), F32)
    for k, line in enumerate(lines):
        extras = jnp.where(entry == k, line, extras)
    mine = mm(chosen, extras.astype(BF16), NT)
    repeat = jnp.where((iota((16, 256), 1) & 15) == iota((16, 256), 0), 1.0, 0.0).astype(BF16)
    mine = mm(mine.astype(BF16), repeat)
    here = iota((total, 256), 0) & 15
    mine = jnp.where((iota((total, 256), 1) >> 4) == here, mine, 0.0)
    mine = jnp.sum(mine.reshape(total // ROWS, ROWS, 256), axis=1, keepdims=True)
    placed = placed.reshape(total // ROWS, ROWS, 256)
    result = jnp.where(iota(placed.shape, 1) == SLOTS, mine, placed)
    out_ref[...] = result.reshape(total, 256).astype(BF16)


def pack(amplitude, tilt, owner, row_offset, col_offset, wide_count):
    count = amplitude.shape[0]
    return pl.pallas_call(
        pack_kernel,
        out_shape=jax.ShapeDtypeStruct((wide_count * ROWS, 256), BF16),
        in_specs=[pl.BlockSpec(memory_space=pltpu.VMEM)] * 5,
        out_specs=pl.BlockSpec(memory_space=pltpu.VMEM),
        compiler_params=pltpu.CompilerParams(vmem_limit_bytes=24 << 20),
        name="pack",
    )(
        amplitude,
        tilt,
        owner.reshape(1, count),
        row_offset.reshape(1, count),
        col_offset.reshape(1, count),
    )


def column_kernel(inc_ref, fblk_ref, grow_ref, *refs):
    outs, (facets_lo, facets_hi, plane, total) = refs[:-4], refs[-4:]
    sources = inc_ref.shape[0] // ROWS
    lanes = CAP * sources
    facets_lo[...] = inc_ref[:, :128].astype(F32)
    facets_hi[...] = inc_ref[:, 128:].astype(F32)
    total[...] = jnp.zeros_like(total)

    def slot(i):
        pick = pl.ds(i, sources, stride=ROWS)
        return jnp.concatenate([facets_lo[pick, :], facets_hi[pick, :]], axis=1)

    extras = slot(SLOTS)
    residue = iota((16, lanes), 0).astype(F32)
    mx = iota((2 * TW, 1), 0) & (TW - 1)

    def one_column(j, carry):
        slots = [CAP * j + k for k in range(CAP)]
        amp = jnp.concatenate([slot(i) for i in slots], axis=0).T
        par = jnp.concatenate(
            [pltpu.roll(extras, 256 - 16 * i, 1)[:, :128] for i in slots], axis=0
        ).T
        tilt = [par[k : k + 1] + par[3 + k : 4 + k] + par[6 + k : 7 + k] for k in range(3)]
        block, turn_u, col = par[9:10], par[10:11], par[11:12]
        turn_v = col - 16.0 * jnp.floor(col * 0.0625)
        u = residue - turn_u
        u = jnp.where(u < 0, u + 16.0, u)
        v = residue - turn_v
        v = jnp.where(v < 0, v + 16.0, v)
        row_r, row_i = cis(tilt[0] * u + tilt[2])
        col_r, col_i = cis(tilt[1] * v)
        block = block + jnp.where(residue < turn_u, 1.0, 0.0)
        ahead = iota((TW, lanes), 0).astype(F32) - col
        window = jnp.where((ahead >= 0) & (ahead < 16.0), 1.0, 0.0).astype(BF16)
        spot = iota((128, lanes), 0)
        for group in range(4):
            part = None
            for member in range(4):
                p = 4 * group + member
                cos_p, sin_p = row_r[p : p + 1], row_i[p : p + 1]
                patch = amp[16 * p : 16 * p + 16]
                real = (patch * (cos_p * col_r - sin_p * col_i)).astype(BF16)
                imag = (patch * (cos_p * col_i + sin_p * col_r)).astype(BF16)
                spread = jnp.concatenate(
                    [jnp.concatenate([real] * 16, axis=0) * window]
                    + [jnp.concatenate([imag] * 16, axis=0) * window],
                    axis=0,
                )
                want = block[p : p + 1] + float(32 * member)
                hot = jnp.where(spot.astype(F32) == want, 1.0, 0.0).astype(BF16)
                term = mm(spread, hot, NT)
                part = term if part is None else part + term
            plane[:, 128 * group : 128 * group + 128] = part.astype(BF16)
        weight = reach_weight(mx, TW, (REACH - j).astype(F32))
        total[...] += weight * mm(fblk_ref[...], plane[...])
        return carry

    lax.fori_loop(0, OFFSETS, one_column, 0)
    rows = TW // len(outs)
    for k, out_ref in enumerate(outs):
        top = mm(total[rows * k : rows * k + rows].astype(BF16), grow_ref[...])
        bottom = mm(total[TW + rows * k : TW + rows * k + rows].astype(BF16), grow_ref[...])
        out_ref[0] = ((top[:, :TH] - bottom[:, TH:]) * SCALE).astype(BF16)
        out_ref[1] = ((top[:, TH:] + bottom[:, :TH]) * SCALE).astype(BF16)


def column_sums(incoming, fblk, grow, chunks):
    piece = jax.ShapeDtypeStruct((2, TW // chunks, TH), BF16)
    return pl.pallas_call(
        column_kernel,
        out_shape=tuple([piece] * chunks),
        in_specs=[pl.BlockSpec(memory_space=pltpu.VMEM)] * 3,
        out_specs=tuple([pl.BlockSpec(memory_space=pltpu.VMEM)] * chunks),
        scratch_shapes=[
            pltpu.VMEM((incoming.shape[0], 128), F32),
            pltpu.VMEM((incoming.shape[0], 128), F32),
            pltpu.VMEM((2 * TW, TH), BF16),
            pltpu.VMEM((2 * TW, TH), F32),
        ],
        compiler_params=pltpu.CompilerParams(vmem_limit_bytes=40 << 20),
        name="column_sums",
    )(incoming, fblk, grow)


def image_kernel(chunks, *refs):
    pieces = refs[: OFFSETS * chunks]
    hblk_ref, kr_ref, ki_ref, out_ref, band = refs[OFFSETS * chunks :]
    my = iota((1, TH), 1)
    rows = TW // chunks
    for part in range(2):
        for k in range(chunks):
            acc = None
            for at in range(OFFSETS):
                piece = pieces[OFFSETS * k + at]
                term = reach_weight(my, TH, float(at - REACH)) * piece[part].astype(F32)
                acc = term if acc is None else acc + term
            start = TW * part + rows * k
            band[start : start + rows, :] = acc.astype(BF16)
    image = mm(hblk_ref[...], band[...]).astype(BF16)
    image_r, image_i = image[:TW], image[TW:]
    out_ref[0] = (mm(kr_ref[...], image_r, NT) - mm(ki_ref[...], image_i, NT)) * SCALE
    out_ref[1] = (mm(kr_ref[...], image_i, NT) + mm(ki_ref[...], image_r, NT)) * SCALE


def image_of(pieces, hblk, kr, ki, chunks):
    return pl.pallas_call(
        functools.partial(image_kernel, chunks),
        out_shape=jax.ShapeDtypeStruct((2, TH, TW), F32),
        in_specs=[pl.BlockSpec(memory_space=pltpu.VMEM)] * (OFFSETS * chunks + 3),
        out_specs=pl.BlockSpec(memory_space=pltpu.VMEM),
        scratch_shapes=[pltpu.VMEM((2 * TW, TH), BF16)],
        compiler_params=pltpu.CompilerParams(vmem_limit_bytes=40 << 20),
        name="image",
    )(*pieces, hblk, kr, ki)


def local(amplitude, tilt, owner, row_offset, col_offset):
    chunks = 2
    wide_count = lax.axis_size("wide")
    fblk, grow, hblk, kr, ki = make_tables()
    outgoing = pack(amplitude, tilt, owner, row_offset, col_offset, wide_count)
    incoming = lax.all_to_all(
        outgoing.reshape(wide_count, ROWS, 256), "wide", split_axis=0, concat_axis=0, tiled=True
    ).reshape(wide_count * ROWS, 256)
    own = column_sums(incoming, fblk, grow, chunks)
    pieces = []
    for mine in own:
        below1 = from_behind(mine, "narrow", 1)
        above1 = from_behind(mine, "narrow", -1)
        below2 = from_behind(below1, "narrow", 1)
        above2 = from_behind(above1, "narrow", -1)
        pieces += [above2, above1, mine, below1, below2]
    return image_of(pieces, hblk, kr, ki, chunks)


def solution(mesh):
    in_specs = (
        P(("wide", "narrow"), None),
        P(None, ("wide", "narrow")),
        P(("wide", "narrow"), None),
        P(("wide", "narrow")),
        P(("wide", "narrow")),
    )
    out_specs = P(None, "narrow", "wide")
    return jax.shard_map(local, mesh=mesh, in_specs=in_specs, out_specs=out_specs, check_vma=False)
```

```python
import functools
import math

import jax
import jax.numpy as jnp
from jax import lax
from jax.experimental import pallas as pl
from jax.experimental.pallas import tpu as pltpu
from jax.sharding import PartitionSpec as P

TH = 512
TW = 256
FACET = 16
DEPTH = 1280
REACH = 2
OFFSETS = 2 * REACH + 1
CAP = 3
SLOTS = OFFSETS * CAP
HALF = TH // 2
ROWS = 16
SPREAD = 16.0
SCALE = 1.0 / math.sqrt(TH * TW)

F32 = jnp.float32
BF16 = jnp.bfloat16
NN = (((1,), (0,)), ((), ()))
NT = (((1,), (1,)), ((), ()))


def mm(a, b, dims=NN):
    return lax.dot_general(a, b, dims, preferred_element_type=F32)


def iota(shape, dim):
    return lax.broadcasted_iota(jnp.int32, shape, dim)


def cis(angle):
    return jnp.cos(angle), jnp.sin(angle)


def signed_frequency(position, length):
    return ((position + length // 2) & (length - 1)) - length // 2


def depth_phase(position, length):
    frequency = signed_frequency(position, length)
    turns = (DEPTH * frequency * frequency) & (2 * length * length - 1)
    return turns.astype(F32) * (-math.pi / (length * length))


def reach_weight(position, length, offset):
    travel = signed_frequency(position, length).astype(F32) * (DEPTH / (length * length))
    return jnp.exp(-((travel - offset) ** 2) / SPREAD)


def turn_angle(a, b, length):
    return ((a * b) & (length - 1)).astype(F32) * (2.0 * math.pi / length)


def table_kernel(fblk_ref, grow_a_ref, grow_b_ref, hblk_ref, kr_a_ref, ki_a_ref, kr_b_ref, ki_b_ref):
    fine_r, fine_i = cis(-turn_angle(iota((16, TW), 0), iota((16, TW), 1), TW))
    wide_r, wide_i = cis(-turn_angle(iota((16, TW), 0), iota((16, TW), 1), 16))
    for a in range(16):
        real = (wide_r[a : a + 1] * fine_r - wide_i[a : a + 1] * fine_i).astype(BF16)
        imag = (wide_r[a : a + 1] * fine_i + wide_i[a : a + 1] * fine_r).astype(BF16)
        at = 16 * a
        fblk_ref[at : at + 16, :TW] = real
        fblk_ref[at : at + 16, TW:] = -imag
        fblk_ref[TW + at : TW + at + 16, :TW] = imag
        fblk_ref[TW + at : TW + at + 16, TW:] = real
    wide_r, wide_i = cis(
        turn_angle(iota((16, TW), 0), iota((16, TW), 1), 16) + depth_phase(iota((16, TW), 1), TW)
    )
    for a in range(16):
        real = (wide_r[a : a + 1] * fine_r + wide_i[a : a + 1] * fine_i).astype(BF16)
        imag = (wide_i[a : a + 1] * fine_r - wide_r[a : a + 1] * fine_i).astype(BF16)
        at = 16 * a
        hblk_ref[at : at + 16, :TW] = real
        hblk_ref[at : at + 16, TW:] = -imag
        hblk_ref[TW + at : TW + at + 16, :TW] = imag
        hblk_ref[TW + at : TW + at + 16, TW:] = real
    fine_r, fine_i = cis(-turn_angle(iota((16, TH), 0), iota((16, TH), 1), TH))
    wide_r, wide_i = cis(-turn_angle(iota((32, TH), 0), iota((32, TH), 1), 32))
    for p in range(16):
        real = (fine_r[p : p + 1] * wide_r - fine_i[p : p + 1] * wide_i).astype(BF16)
        imag = (fine_r[p : p + 1] * wide_i + fine_i[p : p + 1] * wide_r).astype(BF16)
        at = 32 * p
        for k, ref in enumerate((grow_a_ref, grow_b_ref)):
            ref[at : at + 32, :HALF] = real[:, HALF * k : HALF * k + HALF]
            ref[at : at + 32, HALF:] = imag[:, HALF * k : HALF * k + HALF]
    wide_r, wide_i = cis(
        turn_angle(iota((32, TH), 0), iota((32, TH), 1), 32) + depth_phase(iota((32, TH), 1), TH)
    )
    for q in range(32):
        real = (wide_r[q : q + 1] * fine_r + wide_i[q : q + 1] * fine_i).astype(BF16)
        imag = (wide_i[q : q + 1] * fine_r - wide_r[q : q + 1] * fine_i).astype(BF16)
        at = 16 * q
        for k, (r_ref, i_ref) in enumerate(((kr_a_ref, ki_a_ref), (kr_b_ref, ki_b_ref))):
            r_ref[at : at + 16, :] = real[:, HALF * k : HALF * k + HALF]
            i_ref[at : at + 16, :] = imag[:, HALF * k : HALF * k + HALF]


def make_tables():
    square = jax.ShapeDtypeStruct((TH, TH), BF16)
    half = jax.ShapeDtypeStruct((TH, HALF), BF16)
    return pl.pallas_call(
        table_kernel,
        out_shape=(square, square, square, square, half, half, half, half),
        out_specs=tuple([pl.BlockSpec(memory_space=pltpu.VMEM)] * 8),
        compiler_params=pltpu.CompilerParams(vmem_limit_bytes=12 << 20),
        cost_estimate=pl.CostEstimate(flops=8_000_000, bytes_accessed=3 << 20, transcendentals=200_000),
        name="tables",
    )()


def pack_kernel(amp_ref, tilt_ref, owner_ref, row_ref, col_ref, out_ref):
    count = amp_ref.shape[0]
    total = out_ref.shape[0]
    row, col = row_ref[...], col_ref[...]
    owner = owner_ref[...].astype(F32)
    sub, lane = iota((count, count), 0), iota((count, count), 1)

    def upright(vector):
        picked = jnp.where(sub == lane, vector.astype(F32), 0.0)
        return jnp.sum(picked, axis=1, keepdims=True)

    same = (upright(owner) == owner) & (sub < lane)
    rank = jnp.sum(jnp.where(same, 1.0, 0.0), axis=0, keepdims=True)
    key = CAP * owner + rank
    amp = amp_ref[...]
    turn_v = upright(col & 15).astype(jnp.int32)
    turn_u = upright(row & 15).astype(jnp.int32)
    within = iota(amp.shape, 1) & 15
    for step in (1, 2, 4, 8):
        moved = jnp.where(
            within >= step, pltpu.roll(amp, step, 1), pltpu.roll(amp, 240 + step, 1)
        )
        amp = jnp.where((turn_v & step) != 0, moved, amp)
    for step in (1, 2, 4, 8):
        amp = jnp.where((turn_u & step) != 0, pltpu.roll(amp, 16 * step, 1), amp)
    at = iota((total, count), 0)
    wanted = CAP * (at >> 4) + (at & 15) - CAP * REACH
    wanted = jnp.where((at & 15) == SLOTS, -1, wanted).astype(F32)
    chosen = jnp.where(wanted == key, 1.0, 0.0).astype(BF16)
    old = iota((256, 256), 0)
    new = ((old >> 4) & 3) * 64 + (old >> 6) * 16 + (old & 15)
    order = jnp.where(iota((256, 256), 1) == new, 1.0, 0.0).astype(BF16)
    placed = mm(chosen, mm(amp.astype(BF16), order).astype(BF16))
    tilt = tilt_ref[...]
    high = tilt.astype(BF16).astype(F32)
    middle = (tilt - high).astype(BF16).astype(F32)
    low = tilt - high - middle
    lines = [part[k : k + 1] for part in (high, middle, low) for k in range(3)]
    lines += [(row >> 4).astype(F32), (row & 15).astype(F32), col.astype(F32)]
    entry = iota((16, count), 0)
    extras = jnp.zeros((16, count), F32)
    for k, line in enumerate(lines):
        extras = jnp.where(entry == k, line, extras)
    mine = mm(chosen, extras.astype(BF16), NT)
    repeat = jnp.where((iota((16, 256), 1) & 15) == iota((16, 256), 0), 1.0, 0.0).astype(BF16)
    mine = mm(mine.astype(BF16), repeat)
    here = iota((total, 256), 0) & 15
    mine = jnp.where((iota((total, 256), 1) >> 4) == here, mine, 0.0)
    mine = jnp.sum(mine.reshape(total // ROWS, ROWS, 256), axis=1, keepdims=True)
    placed = placed.reshape(total // ROWS, ROWS, 256)
    result = jnp.where(iota(placed.shape, 1) == SLOTS, mine, placed)
    out_ref[...] = result.reshape(total, 256).astype(BF16)


def pack(amplitude, tilt, owner, row_offset, col_offset, wide_count):
    count = amplitude.shape[0]
    return pl.pallas_call(
        pack_kernel,
        out_shape=jax.ShapeDtypeStruct((wide_count * ROWS, 256), BF16),
        in_specs=[pl.BlockSpec(memory_space=pltpu.VMEM)] * 5,
        out_specs=pl.BlockSpec(memory_space=pltpu.VMEM),
        compiler_params=pltpu.CompilerParams(vmem_limit_bytes=63 << 20),
        name="pack",
    )(
        amplitude,
        tilt,
        owner.reshape(1, count),
        row_offset.reshape(1, count),
        col_offset.reshape(1, count),
    )


def power_of(base_r, base_i, exponent, start_r, start_i):
    real, imag = start_r, start_i
    for bit in (1, 2, 4, 8):
        step = (exponent & bit) != 0
        turned_r = real * base_r - imag * base_i
        turned_i = real * base_i + imag * base_r
        real = jnp.where(step, turned_r, real)
        imag = jnp.where(step, turned_i, imag)
        base_r, base_i = base_r * base_r - base_i * base_i, 2.0 * base_r * base_i
    return real, imag


def row_transform(value, grow_ref, out_ref):
    product = mm(value, grow_ref[...])
    out_ref[0] = ((product[:TW, :HALF] - product[TW:, HALF:]) * SCALE).astype(BF16)
    out_ref[1] = ((product[:TW, HALF:] + product[TW:, :HALF]) * SCALE).astype(BF16)


def column_kernel(inc_ref, fblk_ref, grow_ref, out_ref, value_ref, facets_lo, facets_hi, param, plane, total):
    sources = inc_ref.shape[0] // ROWS
    lanes = 4 * sources
    facets_lo[...] = inc_ref[:, :128].astype(F32)
    facets_hi[...] = inc_ref[:, 128:].astype(F32)
    total[...] = jnp.zeros_like(total)
    pick = pl.ds(SLOTS, sources, stride=ROWS)
    extras = jnp.concatenate([facets_lo[pick, :], facets_hi[pick, :]], axis=1)
    entry = iota(extras.shape, 1) & 15
    tilt = extras + pltpu.roll(extras, 253, 1) + pltpu.roll(extras, 250, 1)
    tilt = jnp.where(entry < 3, tilt, pltpu.roll(tilt, 3, 1))
    turn_r, turn_i = cis(tilt)
    param[...] = jnp.where(entry < 3, turn_r, jnp.where(entry < 6, turn_i, extras))
    mx = iota((2 * TW, 1), 0) & (TW - 1)
    member = iota((8, lanes), 1) // sources
    residue = 4 * iota((8, lanes), 0) + member
    spot = iota((128, lanes), 0).astype(F32)
    aside = iota((sources, 128), 1) < 64

    def one_slot(i):
        pick = pl.ds(i, sources, stride=ROWS)
        low, high = facets_lo[pick, :], facets_hi[pick, :]
        mine = pltpu.roll(param[...], (320 - 16 * i) & 255, 1)[:, :128]
        blocks = [low, pltpu.roll(low, 64, 1), high, pltpu.roll(high, 64, 1)]
        turned = jnp.concatenate([jnp.where(aside, block, mine) for block in blocks], axis=0).T
        par = turned[64:80]
        block, turn_u, col = [par[k : k + 1].astype(jnp.int32) for k in (9, 10, 11)]
        row_r, row_i = power_of(
            par[0:1], par[3:4], (residue - turn_u) & 15, par[2:3], par[5:6]
        )
        one = jnp.ones((16, lanes), F32)
        col_r, col_i = power_of(
            par[1:2], par[4:5], (iota((16, lanes), 0) - col) & 15, one, one * 0.0
        )
        spots = (block + jnp.where(residue < turn_u, 1, 0) + 32 * member).astype(F32)
        ahead = iota((TW, lanes), 0) - col
        window = jnp.where((ahead & -16) == 0, 1.0, 0.0).astype(BF16)
        return turned, row_r, row_i, col_r, col_i, spots, window

    def one_column(j, carry):
        slots = [one_slot(CAP * j + k) for k in range(CAP)]
        for group in range(4):
            spreads, hots = [], []
            for turned, row_r, row_i, col_r, col_i, spots, window in slots:
                patch = turned[16 * group : 16 * group + 16]
                cos_p, sin_p = row_r[group : group + 1], row_i[group : group + 1]
                real = (patch * (cos_p * col_r - sin_p * col_i)).astype(BF16)
                imag = (patch * (cos_p * col_i + sin_p * col_r)).astype(BF16)
                spreads.append(
                    jnp.concatenate(
                        [jnp.concatenate([real] * 16, axis=0) * window]
                        + [jnp.concatenate([imag] * 16, axis=0) * window],
                        axis=0,
                    )
                )
                hots.append(
                    jnp.where(spot == spots[group : group + 1], 1.0, 0.0).astype(BF16)
                )
            spread = jnp.concatenate(spreads, axis=1)
            hot = jnp.concatenate(hots, axis=1)
            plane[:, 128 * group : 128 * group + 128] = mm(spread, hot, NT).astype(BF16)
        weight = reach_weight(mx, TW, float(REACH - j))
        total[...] += weight * mm(fblk_ref[...], plane[...])
        return carry

    for j in range(OFFSETS):
        one_column(j, 0)
    value = total[...].astype(BF16)
    value_ref[...] = value
    row_transform(value, grow_ref, out_ref)


def column_sums(incoming, fblk, grow):
    return pl.pallas_call(
        column_kernel,
        out_shape=(
            jax.ShapeDtypeStruct((2, TW, HALF), BF16),
            jax.ShapeDtypeStruct((2 * TW, TH), BF16),
        ),
        in_specs=[pl.BlockSpec(memory_space=pltpu.VMEM)] * 3,
        out_specs=tuple([pl.BlockSpec(memory_space=pltpu.VMEM)] * 2),
        scratch_shapes=[
            pltpu.VMEM((incoming.shape[0], 128), F32),
            pltpu.VMEM((incoming.shape[0], 128), F32),
            pltpu.VMEM((incoming.shape[0] // ROWS, 256), F32),
            pltpu.VMEM((2 * TW, TH), BF16),
            pltpu.VMEM((2 * TW, TH), F32),
        ],
        compiler_params=pltpu.CompilerParams(vmem_limit_bytes=20 << 20),
        cost_estimate=pl.CostEstimate(flops=6_000_000_000, bytes_accessed=3 << 20, transcendentals=40_000),
        name="column_sums",
    )(incoming, fblk, grow)


def second_kernel(value_ref, grow_ref, out_ref):
    row_transform(value_ref[...], grow_ref, out_ref)


def second_half(value, grow):
    return pl.pallas_call(
        second_kernel,
        out_shape=jax.ShapeDtypeStruct((2, TW, HALF), BF16),
        in_specs=[pl.BlockSpec(memory_space=pltpu.VMEM)] * 2,
        out_specs=pl.BlockSpec(memory_space=pltpu.VMEM),
        compiler_params=pltpu.CompilerParams(vmem_limit_bytes=8 << 20),
        cost_estimate=pl.CostEstimate(flops=600_000_000, bytes_accessed=2 << 20, transcendentals=0),
        name="second_half",
    )(value, grow)


def image_kernel(half, *refs):
    side = (1 - 2 * (lax.axis_index("narrow") & 1)).astype(F32)
    pieces = refs[:OFFSETS]
    hblk_ref, kr_ref, ki_ref = refs[OFFSETS : OFFSETS + 3]
    before, out_ref, band = refs[OFFSETS + 3 : -2], refs[-2], refs[-1]
    my = iota((1, HALF), 1) + HALF * half
    weights = [reach_weight(my, TH, side * float(REACH - at)) for at in range(OFFSETS)]
    for part in range(2):
        acc = None
        for weight, piece in zip(weights, pieces):
            term = weight * piece[part].astype(F32)
            acc = term if acc is None else acc + term
        band[TW * part : TW * part + TW, :] = acc.astype(BF16)
    image = mm(hblk_ref[...], band[...]).astype(BF16)
    image_r, image_i = image[:TW], image[TW:]
    real = (mm(kr_ref[...], image_r, NT) - mm(ki_ref[...], image_i, NT)) * SCALE
    imag = (mm(kr_ref[...], image_i, NT) + mm(ki_ref[...], image_r, NT)) * SCALE
    if before:
        real = real + before[0][0]
        imag = imag + before[0][1]
    out_ref[0] = real
    out_ref[1] = imag


def image_of(half, pieces, tables, before):
    operands = (*pieces, *tables, *before)
    return pl.pallas_call(
        functools.partial(image_kernel, half),
        out_shape=jax.ShapeDtypeStruct((2, TH, TW), F32),
        in_specs=[pl.BlockSpec(memory_space=pltpu.VMEM)] * len(operands),
        out_specs=pl.BlockSpec(memory_space=pltpu.VMEM),
        scratch_shapes=[pltpu.VMEM((2 * TW, HALF), BF16)],
        compiler_params=pltpu.CompilerParams(vmem_limit_bytes=16 << 20),
        cost_estimate=pl.CostEstimate(flops=900_000_000, bytes_accessed=4 << 20, transcendentals=0),
        name="image",
    )(*operands)


def swap(value, first):
    count = lax.axis_size("narrow")
    pairs = [(low, low + 1) for low in range(first, count - 1, 2)]
    return lax.ppermute(value, "narrow", pairs + [(high, low) for low, high in pairs])


def narrow_pieces(mine):
    above1 = swap(mine, 0)
    below1 = swap(mine, 1)
    above2 = swap(below1, 0)
    below2 = swap(above1, 1)
    return [below2, below1, mine, above1, above2]


def local(amplitude, tilt, owner, row_offset, col_offset):
    wide_count = lax.axis_size("wide")
    fblk, grow_a, grow_b, hblk, kr_a, ki_a, kr_b, ki_b = make_tables()
    outgoing = pack(amplitude, tilt, owner, row_offset, col_offset, wide_count)
    incoming = lax.all_to_all(
        outgoing.reshape(wide_count, ROWS, 256), "wide", split_axis=0, concat_axis=0, tiled=True
    ).reshape(wide_count * ROWS, 256)
    first, value = column_sums(incoming, fblk, grow_a)
    second = second_half(value, grow_b)
    partial = image_of(0, narrow_pieces(first), (hblk, kr_a, ki_a), ())
    return image_of(1, narrow_pieces(second), (hblk, kr_b, ki_b), (partial,))


def solution(mesh):
    in_specs = (
        P(("wide", "narrow"), None),
        P(None, ("wide", "narrow")),
        P(("wide", "narrow"), None),
        P(("wide", "narrow")),
        P(("wide", "narrow")),
    )
    out_specs = P(None, "narrow", "wide")
    return jax.shard_map(local, mesh=mesh, in_specs=in_specs, out_specs=out_specs, check_vma=False)
```

```python
import functools
import math

import jax
import jax.numpy as jnp
from jax import lax
from jax.experimental import pallas as pl
from jax.experimental.pallas import tpu as pltpu
from jax.sharding import PartitionSpec as P

TH = 512
TW = 256
FACET = 16
DEPTH = 1280
REACH = 2
OFFSETS = 2 * REACH + 1
CAP = 3
SLOTS = OFFSETS * CAP
HALF = TH // 2
PARTS = 4
ROWS = 16
SPREAD = 16.0
SCALE = 1.0 / math.sqrt(TH * TW)

F32 = jnp.float32
BF16 = jnp.bfloat16
NN = (((1,), (0,)), ((), ()))
NT = (((1,), (1,)), ((), ()))


def mm(a, b, dims=NN):
    return lax.dot_general(a, b, dims, preferred_element_type=F32)


def iota(shape, dim):
    return lax.broadcasted_iota(jnp.int32, shape, dim)


def cis(angle):
    return jnp.cos(angle), jnp.sin(angle)


def signed_frequency(position, length):
    return ((position + length // 2) & (length - 1)) - length // 2


def depth_phase(position, length):
    frequency = signed_frequency(position, length)
    turns = (DEPTH * frequency * frequency) & (2 * length * length - 1)
    return turns.astype(F32) * (-math.pi / (length * length))


def reach_weight(position, length, offset):
    travel = signed_frequency(position, length).astype(F32) * (DEPTH / (length * length))
    return jnp.exp(-((travel - offset) ** 2) / SPREAD)


def turn_angle(a, b, length):
    return ((a * b) & (length - 1)).astype(F32) * (2.0 * math.pi / length)


def table_kernel(lead_ref, grow_b_ref, hblk_ref, kr_a_ref, ki_a_ref, kr_b_ref, ki_b_ref):
    fblk_ref, grow_a_ref = lead_ref.at[:TH], lead_ref.at[TH:]
    fine_r, fine_i = cis(-turn_angle(iota((16, TW), 0), iota((16, TW), 1), TW))
    wide_r, wide_i = cis(-turn_angle(iota((16, TW), 0), iota((16, TW), 1), 16))
    for a in range(16):
        real = (wide_r[a : a + 1] * fine_r - wide_i[a : a + 1] * fine_i).astype(BF16)
        imag = (wide_r[a : a + 1] * fine_i + wide_i[a : a + 1] * fine_r).astype(BF16)
        at = 16 * a
        fblk_ref[at : at + 16, :TW] = real
        fblk_ref[at : at + 16, TW:] = -imag
        fblk_ref[TW + at : TW + at + 16, :TW] = imag
        fblk_ref[TW + at : TW + at + 16, TW:] = real
    wide_r, wide_i = cis(
        turn_angle(iota((16, TW), 0), iota((16, TW), 1), 16) + depth_phase(iota((16, TW), 1), TW)
    )
    for a in range(16):
        real = (wide_r[a : a + 1] * fine_r + wide_i[a : a + 1] * fine_i).astype(BF16)
        imag = (wide_i[a : a + 1] * fine_r - wide_r[a : a + 1] * fine_i).astype(BF16)
        at = 16 * a
        hblk_ref[at : at + 16, :TW] = real
        hblk_ref[at : at + 16, TW:] = -imag
        hblk_ref[TW + at : TW + at + 16, :TW] = imag
        hblk_ref[TW + at : TW + at + 16, TW:] = real
    fine_r, fine_i = cis(-turn_angle(iota((16, TH), 0), iota((16, TH), 1), TH))
    wide_r, wide_i = cis(-turn_angle(iota((32, TH), 0), iota((32, TH), 1), 32))
    for p in range(16):
        real = (fine_r[p : p + 1] * wide_r - fine_i[p : p + 1] * wide_i).astype(BF16)
        imag = (fine_r[p : p + 1] * wide_i + fine_i[p : p + 1] * wide_r).astype(BF16)
        at = 32 * p
        for k, ref in enumerate((grow_a_ref, grow_b_ref)):
            ref[at : at + 32, :HALF] = real[:, HALF * k : HALF * k + HALF]
            ref[at : at + 32, HALF:] = imag[:, HALF * k : HALF * k + HALF]
    wide_r, wide_i = cis(
        turn_angle(iota((32, TH), 0), iota((32, TH), 1), 32) + depth_phase(iota((32, TH), 1), TH)
    )
    for q in range(32):
        real = (wide_r[q : q + 1] * fine_r + wide_i[q : q + 1] * fine_i).astype(BF16)
        imag = (wide_i[q : q + 1] * fine_r - wide_r[q : q + 1] * fine_i).astype(BF16)
        at = 16 * q
        for k, (r_ref, i_ref) in enumerate(((kr_a_ref, ki_a_ref), (kr_b_ref, ki_b_ref))):
            r_ref[at : at + 16, :] = real[:, HALF * k : HALF * k + HALF]
            i_ref[at : at + 16, :] = imag[:, HALF * k : HALF * k + HALF]


def make_tables():
    square = jax.ShapeDtypeStruct((TH, TH), BF16)
    half = jax.ShapeDtypeStruct((TH, HALF), BF16)
    return pl.pallas_call(
        table_kernel,
        out_shape=(jax.ShapeDtypeStruct((2 * TH, TH), BF16), square, square, half, half, half, half),
        out_specs=tuple([pl.BlockSpec(memory_space=pltpu.VMEM)] * 7),
        compiler_params=pltpu.CompilerParams(vmem_limit_bytes=12 << 20),
        cost_estimate=pl.CostEstimate(flops=8_000_000, bytes_accessed=3 << 20, transcendentals=200_000),
        name="tables",
    )()


def pack_kernel(amp_at, tilt_at, owner_at, row_at, col_at, out_at, *scratch):
    amp_ref, tilt_ref, owner_ref, row_ref, col_ref, out_ref, sems, out_sems = scratch
    copies = [
        pltpu.make_async_copy(place, ref, sems.at[k])
        for k, (place, ref) in enumerate(
            (
                (owner_at, owner_ref),
                (row_at, row_ref),
                (col_at, col_ref),
                (tilt_at, tilt_ref),
                (amp_at, amp_ref),
            )
        )
    ]
    for copy in copies:
        copy.start()
    count = amp_ref.shape[0]
    total = out_ref.shape[0]
    sub, lane = iota((count, count), 0), iota((count, count), 1)
    at = iota((total, count), 0)
    wanted = CAP * (at >> 4) + (at & 15) - CAP * REACH
    wanted = jnp.where((at & 15) == SLOTS, -1, wanted).astype(F32)
    old = iota((256, 256), 0)
    new = ((old >> 4) & 3) * 64 + (old >> 6) * 16 + (old & 15)
    order = jnp.where(iota((256, 256), 1) == new, 1.0, 0.0).astype(BF16)
    repeat = jnp.where((iota((16, 256), 1) & 15) == iota((16, 256), 0), 1.0, 0.0).astype(BF16)
    for copy in copies:
        copy.wait()
    row, col = row_ref[...], col_ref[...]
    owner = owner_ref[...].astype(F32)

    def upright(vector):
        picked = jnp.where(sub == lane, vector.astype(F32), 0.0)
        return jnp.sum(picked, axis=1, keepdims=True)

    same = (upright(owner) == owner) & (sub < lane)
    rank = jnp.sum(jnp.where(same, 1.0, 0.0), axis=0, keepdims=True)
    key = CAP * owner + rank
    chosen = jnp.where(wanted == key, 1.0, 0.0).astype(BF16)
    amp = amp_ref[...]
    turn_v = upright(col & 15).astype(jnp.int32)
    turn_u = upright(row & 15).astype(jnp.int32)
    within = iota(amp.shape, 1) & 15
    for step in (1, 2, 4, 8):
        moved = jnp.where(
            within >= step, pltpu.roll(amp, step, 1), pltpu.roll(amp, 240 + step, 1)
        )
        amp = jnp.where((turn_v & step) != 0, moved, amp)
    for step in (1, 2, 4, 8):
        amp = jnp.where((turn_u & step) != 0, pltpu.roll(amp, 16 * step, 1), amp)
    amp = mm(amp.astype(BF16), order).astype(BF16)
    tilt = tilt_ref[...]
    high = tilt.astype(BF16).astype(F32)
    middle = (tilt - high).astype(BF16).astype(F32)
    low = tilt - high - middle
    lines = [part[k : k + 1] for part in (high, middle, low) for k in range(3)]
    lines += [(row >> 4).astype(F32), (row & 15).astype(F32), col.astype(F32)]
    entry = iota((16, count), 0)
    extras = jnp.zeros((16, count), F32)
    for k, line in enumerate(lines):
        extras = jnp.where(entry == k, line, extras)
    extras = lax.dot_general(
        extras.astype(BF16), repeat, (((0,), (0,)), ((), ())), preferred_element_type=F32
    ).astype(BF16)
    both = jnp.concatenate([amp, extras], axis=1)
    part = total // PARTS
    keep = (iota((part, 256), 1) >> 4) == (iota((part, 256), 0) & 15)
    last = iota((part // ROWS, ROWS, 256), 1) == SLOTS
    sends = []
    for k in range(PARTS):
        rows = pl.ds(part * k, part)
        found = mm(chosen[part * k : part * k + part], both)
        placed = found[:, :256].reshape(part // ROWS, ROWS, 256)
        mine = jnp.where(keep, found[:, 256:], 0.0).reshape(part // ROWS, ROWS, 256)
        mine = jnp.sum(mine, axis=1, keepdims=True)
        out_ref[rows, :] = jnp.where(last, mine, placed).reshape(part, 256).astype(BF16)
        send = pltpu.make_async_copy(out_ref.at[rows], out_at.at[rows], out_sems.at[k])
        send.start()
        sends.append(send)
    for send in sends:
        send.wait()


def pack(amplitude, tilt, owner, row_offset, col_offset, wide_count):
    count = amplitude.shape[0]
    return pl.pallas_call(
        pack_kernel,
        out_shape=jax.ShapeDtypeStruct((wide_count * ROWS, 256), BF16),
        in_specs=[pl.BlockSpec(memory_space=pl.ANY)] * 5,
        out_specs=pl.BlockSpec(memory_space=pl.ANY),
        scratch_shapes=[
            pltpu.VMEM((count, 256), F32),
            pltpu.VMEM((3, count), F32),
            pltpu.VMEM((1, count), jnp.int32),
            pltpu.VMEM((1, count), jnp.int32),
            pltpu.VMEM((1, count), jnp.int32),
            pltpu.VMEM((wide_count * ROWS, 256), BF16),
            pltpu.SemaphoreType.DMA((5,)),
            pltpu.SemaphoreType.DMA((PARTS,)),
        ],
        compiler_params=pltpu.CompilerParams(vmem_limit_bytes=63 << 20),
        name="pack",
    )(
        amplitude,
        tilt,
        owner.reshape(1, count),
        row_offset.reshape(1, count),
        col_offset.reshape(1, count),
    )


def power_of(base_r, base_i, exponent, start_r, start_i):
    real, imag = start_r, start_i
    for bit in (1, 2, 4, 8):
        step = (exponent & bit) != 0
        turned_r = real * base_r - imag * base_i
        turned_i = real * base_i + imag * base_r
        real = jnp.where(step, turned_r, real)
        imag = jnp.where(step, turned_i, imag)
        base_r, base_i = base_r * base_r - base_i * base_i, 2.0 * base_r * base_i
    return real, imag


def row_transform(value, grow_ref, out_ref):
    product = mm(value, grow_ref[...])
    out_ref[0] = ((product[:TW, :HALF] - product[TW:, HALF:]) * SCALE).astype(BF16)
    out_ref[1] = ((product[:TW, HALF:] + product[TW:, :HALF]) * SCALE).astype(BF16)


def column_kernel(inc_ref, lead_ref, out_ref, value_ref, facets_lo, facets_hi, param, plane, total):
    fblk_ref, grow_ref = lead_ref.at[:TH], lead_ref.at[TH:]
    sources = inc_ref.shape[0] // ROWS
    lanes = 4 * sources
    facets_lo[...] = inc_ref[:, :128].astype(F32)
    facets_hi[...] = inc_ref[:, 128:].astype(F32)
    total[...] = jnp.zeros_like(total)
    pick = pl.ds(SLOTS, sources, stride=ROWS)
    extras = jnp.concatenate([facets_lo[pick, :], facets_hi[pick, :]], axis=1)
    entry = iota(extras.shape, 1) & 15
    tilt = extras + pltpu.roll(extras, 253, 1) + pltpu.roll(extras, 250, 1)
    tilt = jnp.where(entry < 3, tilt, pltpu.roll(tilt, 3, 1))
    turn_r, turn_i = cis(tilt)
    param[...] = jnp.where(entry < 3, turn_r, jnp.where(entry < 6, turn_i, extras))
    mx = iota((2 * TW, 1), 0) & (TW - 1)
    member = iota((8, lanes), 1) // sources
    residue = 4 * iota((8, lanes), 0) + member
    spot = iota((128, lanes), 0).astype(F32)
    aside = iota((sources, 128), 1) < 64

    def one_slot(i):
        pick = pl.ds(i, sources, stride=ROWS)
        low, high = facets_lo[pick, :], facets_hi[pick, :]
        mine = pltpu.roll(param[...], (320 - 16 * i) & 255, 1)[:, :128]
        blocks = [low, pltpu.roll(low, 64, 1), high, pltpu.roll(high, 64, 1)]
        turned = jnp.concatenate([jnp.where(aside, block, mine) for block in blocks], axis=0).T
        par = turned[64:80]
        block, turn_u, col = [par[k : k + 1].astype(jnp.int32) for k in (9, 10, 11)]
        row_r, row_i = power_of(
            par[0:1], par[3:4], (residue - turn_u) & 15, par[2:3], par[5:6]
        )
        one = jnp.ones((16, lanes), F32)
        col_r, col_i = power_of(
            par[1:2], par[4:5], (iota((16, lanes), 0) - col) & 15, one, one * 0.0
        )
        spots = (block + jnp.where(residue < turn_u, 1, 0) + 32 * member).astype(F32)
        ahead = iota((TW, lanes), 0) - col
        window = jnp.where((ahead & -16) == 0, 1.0, 0.0).astype(BF16)
        return turned, row_r, row_i, col_r, col_i, spots, window

    def one_column(j, carry):
        slots = [one_slot(CAP * j + k) for k in range(CAP)]
        for group in range(4):
            spreads, hots = [], []
            for turned, row_r, row_i, col_r, col_i, spots, window in slots:
                patch = turned[16 * group : 16 * group + 16]
                cos_p, sin_p = row_r[group : group + 1], row_i[group : group + 1]
                real = (patch * (cos_p * col_r - sin_p * col_i)).astype(BF16)
                imag = (patch * (cos_p * col_i + sin_p * col_r)).astype(BF16)
                spreads.append(
                    jnp.concatenate(
                        [jnp.concatenate([real] * 16, axis=0) * window]
                        + [jnp.concatenate([imag] * 16, axis=0) * window],
                        axis=0,
                    )
                )
                hots.append(
                    jnp.where(spot == spots[group : group + 1], 1.0, 0.0).astype(BF16)
                )
            spread = jnp.concatenate(spreads, axis=1)
            hot = jnp.concatenate(hots, axis=1)
            plane[:, 128 * group : 128 * group + 128] = mm(spread, hot, NT).astype(BF16)
        weight = reach_weight(mx, TW, float(REACH - j))
        total[...] += weight * mm(fblk_ref[...], plane[...])
        return carry

    for j in range(OFFSETS):
        one_column(j, 0)
    value = total[...].astype(BF16)
    value_ref[...] = value
    row_transform(value, grow_ref, out_ref)


def column_sums(incoming, lead):
    return pl.pallas_call(
        column_kernel,
        out_shape=(
            jax.ShapeDtypeStruct((2, TW, HALF), BF16),
            jax.ShapeDtypeStruct((2 * TW, TH), BF16),
        ),
        in_specs=[pl.BlockSpec(memory_space=pltpu.VMEM)] * 2,
        out_specs=tuple([pl.BlockSpec(memory_space=pltpu.VMEM)] * 2),
        scratch_shapes=[
            pltpu.VMEM((incoming.shape[0], 128), F32),
            pltpu.VMEM((incoming.shape[0], 128), F32),
            pltpu.VMEM((incoming.shape[0] // ROWS, 256), F32),
            pltpu.VMEM((2 * TW, TH), BF16),
            pltpu.VMEM((2 * TW, TH), F32),
        ],
        compiler_params=pltpu.CompilerParams(vmem_limit_bytes=20 << 20),
        cost_estimate=pl.CostEstimate(flops=6_000_000_000, bytes_accessed=3 << 20, transcendentals=40_000),
        name="column_sums",
    )(incoming, lead)


def second_kernel(value_ref, grow_ref, out_ref):
    row_transform(value_ref[...], grow_ref, out_ref)


def second_half(value, grow):
    return pl.pallas_call(
        second_kernel,
        out_shape=jax.ShapeDtypeStruct((2, TW, HALF), BF16),
        in_specs=[pl.BlockSpec(memory_space=pltpu.VMEM)] * 2,
        out_specs=pl.BlockSpec(memory_space=pltpu.VMEM),
        compiler_params=pltpu.CompilerParams(vmem_limit_bytes=8 << 20),
        cost_estimate=pl.CostEstimate(flops=600_000_000, bytes_accessed=2 << 20, transcendentals=0),
        name="second_half",
    )(value, grow)


def image_kernel(half, *refs):
    side = (1 - 2 * (lax.axis_index("narrow") & 1)).astype(F32)
    pieces = refs[:OFFSETS]
    hblk_ref, kr_ref, ki_ref = refs[OFFSETS : OFFSETS + 3]
    my = iota((1, HALF), 1) + HALF * half
    weights = [reach_weight(my, TH, side * float(REACH - at)) for at in range(OFFSETS)]

    def band(part):
        acc = None
        for weight, piece in zip(weights, pieces):
            term = weight * piece[part].astype(F32)
            acc = term if acc is None else acc + term
        return acc.astype(BF16)

    image = mm(hblk_ref[...], jnp.concatenate([band(0), band(1)], axis=0)).astype(BF16)
    image_r, image_i = image[:TW], image[TW:]

    def share(rows, part):
        kr, ki = kr_ref[rows, :], ki_ref[rows, :]
        if part == 0:
            return (mm(kr, image_r, NT) - mm(ki, image_i, NT)) * SCALE
        return (mm(kr, image_i, NT) + mm(ki, image_r, NT)) * SCALE

    if half == 0:
        out_ref = refs[OFFSETS + 3]
        for part in range(2):
            out_ref[part] = share(pl.ds(0, TH), part)
        return
    before, out_at, out_ref, sems = refs[OFFSETS + 3 :]
    sends = []
    step = TH // 2
    for k in range(4):
        part, rows = k // 2, pl.ds(step * (k % 2), step)
        out_ref[part, rows, :] = share(rows, part) + before[part, rows, :]
        send = pltpu.make_async_copy(
            out_ref.at[part, rows], out_at.at[part, rows], sems.at[k]
        )
        send.start()
        sends.append(send)
    for send in sends:
        send.wait()


def image_of(half, pieces, tables, before):
    operands = (*pieces, *tables, *before)
    place = pl.ANY if half else pltpu.VMEM
    scratch = [pltpu.VMEM((2, TH, TW), F32), pltpu.SemaphoreType.DMA((4,))] if half else []
    return pl.pallas_call(
        functools.partial(image_kernel, half),
        out_shape=jax.ShapeDtypeStruct((2, TH, TW), F32),
        in_specs=[pl.BlockSpec(memory_space=pltpu.VMEM)] * len(operands),
        out_specs=pl.BlockSpec(memory_space=place),
        scratch_shapes=scratch,
        compiler_params=pltpu.CompilerParams(vmem_limit_bytes=16 << 20),
        cost_estimate=pl.CostEstimate(flops=900_000_000, bytes_accessed=4 << 20, transcendentals=0),
        name="image",
    )(*operands)


def swap(value, first):
    count = lax.axis_size("narrow")
    pairs = [(low, low + 1) for low in range(first, count - 1, 2)]
    return lax.ppermute(value, "narrow", pairs + [(high, low) for low, high in pairs])


def narrow_pieces(mine):
    above1 = swap(mine, 0)
    below1 = swap(mine, 1)
    above2 = swap(below1, 0)
    below2 = swap(above1, 1)
    return [below2, below1, mine, above1, above2]


def local(amplitude, tilt, owner, row_offset, col_offset):
    wide_count = lax.axis_size("wide")
    lead, grow_b, hblk, kr_a, ki_a, kr_b, ki_b = make_tables()
    outgoing = pack(amplitude, tilt, owner, row_offset, col_offset, wide_count)
    incoming = lax.all_to_all(
        outgoing.reshape(wide_count, ROWS, 256), "wide", split_axis=0, concat_axis=0, tiled=True
    ).reshape(wide_count * ROWS, 256)
    first, value = column_sums(incoming, lead)
    second = second_half(value, grow_b)
    partial = image_of(0, narrow_pieces(first), (hblk, kr_a, ki_a), ())
    return image_of(1, narrow_pieces(second), (hblk, kr_b, ki_b), (partial,))


def solution(mesh):
    in_specs = (
        P(("wide", "narrow"), None),
        P(None, ("wide", "narrow")),
        P(("wide", "narrow"), None),
        P(("wide", "narrow")),
        P(("wide", "narrow")),
    )
    out_specs = P(None, "narrow", "wide")
    return jax.shard_map(local, mesh=mesh, in_specs=in_specs, out_specs=out_specs, check_vma=False)
```

```python
import functools
import math

import jax
import jax.numpy as jnp
from jax import lax
from jax.experimental import pallas as pl
from jax.experimental.pallas import tpu as pltpu
from jax.sharding import PartitionSpec as P

TH = 512
TW = 256
FACET = 16
DEPTH = 1280
REACH = 2
OFFSETS = 2 * REACH + 1
CAP = 3
SLOTS = (OFFSETS + 1) * CAP
HALF = TH // 2
PARTS = 4
ROWS = 24
WORDS = 14
SPREAD = 16.0
SCALE = 1.0 / math.sqrt(TH * TW)

F32 = jnp.float32
BF16 = jnp.bfloat16
NN = (((1,), (0,)), ((), ()))
NT = (((1,), (1,)), ((), ()))


def mm(a, b, dims=NN):
    return lax.dot_general(a, b, dims, preferred_element_type=F32)


def iota(shape, dim):
    return lax.broadcasted_iota(jnp.int32, shape, dim)


def cis(angle):
    return jnp.cos(angle), jnp.sin(angle)


def signed_frequency(position, length):
    return ((position + length // 2) & (length - 1)) - length // 2


def depth_phase(position, length):
    frequency = signed_frequency(position, length)
    turns = (DEPTH * frequency * frequency) & (2 * length * length - 1)
    return turns.astype(F32) * (-math.pi / (length * length))


def reach_weight(position, length, offset):
    travel = signed_frequency(position, length).astype(F32) * (DEPTH / (length * length))
    return jnp.exp(-((travel - offset) ** 2) / SPREAD)


def turn_angle(a, b, length):
    return ((a * b) & (length - 1)).astype(F32) * (2.0 * math.pi / length)


def table_kernel(lead_ref, grow_b_ref, hblk_ref, kr_a_ref, ki_a_ref, kr_b_ref, ki_b_ref):
    fblk_ref, grow_a_ref = lead_ref.at[:TH], lead_ref.at[TH:]
    fine_r, fine_i = cis(-turn_angle(iota((16, TW), 0), iota((16, TW), 1), TW))
    wide_r, wide_i = cis(-turn_angle(iota((16, TW), 0), iota((16, TW), 1), 16))
    for a in range(16):
        real = (wide_r[a : a + 1] * fine_r - wide_i[a : a + 1] * fine_i).astype(BF16)
        imag = (wide_r[a : a + 1] * fine_i + wide_i[a : a + 1] * fine_r).astype(BF16)
        at = 16 * a
        fblk_ref[at : at + 16, :TW] = real
        fblk_ref[at : at + 16, TW:] = -imag
        fblk_ref[TW + at : TW + at + 16, :TW] = imag
        fblk_ref[TW + at : TW + at + 16, TW:] = real
    wide_r, wide_i = cis(
        turn_angle(iota((16, TW), 0), iota((16, TW), 1), 16) + depth_phase(iota((16, TW), 1), TW)
    )
    for a in range(16):
        real = (wide_r[a : a + 1] * fine_r + wide_i[a : a + 1] * fine_i).astype(BF16)
        imag = (wide_i[a : a + 1] * fine_r - wide_r[a : a + 1] * fine_i).astype(BF16)
        at = 16 * a
        hblk_ref[at : at + 16, :TW] = real
        hblk_ref[at : at + 16, TW:] = -imag
        hblk_ref[TW + at : TW + at + 16, :TW] = imag
        hblk_ref[TW + at : TW + at + 16, TW:] = real
    fine_r, fine_i = cis(-turn_angle(iota((16, TH), 0), iota((16, TH), 1), TH))
    wide_r, wide_i = cis(-turn_angle(iota((32, TH), 0), iota((32, TH), 1), 32))
    for p in range(16):
        real = (fine_r[p : p + 1] * wide_r - fine_i[p : p + 1] * wide_i).astype(BF16)
        imag = (fine_r[p : p + 1] * wide_i + fine_i[p : p + 1] * wide_r).astype(BF16)
        at = 32 * p
        for k, ref in enumerate((grow_a_ref, grow_b_ref)):
            ref[at : at + 32, :HALF] = real[:, HALF * k : HALF * k + HALF]
            ref[at : at + 32, HALF:] = imag[:, HALF * k : HALF * k + HALF]
    wide_r, wide_i = cis(
        turn_angle(iota((32, TH), 0), iota((32, TH), 1), 32) + depth_phase(iota((32, TH), 1), TH)
    )
    for q in range(32):
        real = (wide_r[q : q + 1] * fine_r + wide_i[q : q + 1] * fine_i).astype(BF16)
        imag = (wide_i[q : q + 1] * fine_r - wide_r[q : q + 1] * fine_i).astype(BF16)
        at = 16 * q
        for k, (r_ref, i_ref) in enumerate(((kr_a_ref, ki_a_ref), (kr_b_ref, ki_b_ref))):
            r_ref[at : at + 16, :] = real[:, HALF * k : HALF * k + HALF]
            i_ref[at : at + 16, :] = imag[:, HALF * k : HALF * k + HALF]


def make_tables():
    square = jax.ShapeDtypeStruct((TH, TH), BF16)
    half = jax.ShapeDtypeStruct((TH, HALF), BF16)
    return pl.pallas_call(
        table_kernel,
        out_shape=(jax.ShapeDtypeStruct((2 * TH, TH), BF16), square, square, half, half, half, half),
        out_specs=tuple([pl.BlockSpec(memory_space=pltpu.VMEM)] * 7),
        compiler_params=pltpu.CompilerParams(vmem_limit_bytes=12 << 20),
        cost_estimate=pl.CostEstimate(flops=8_000_000, bytes_accessed=3 << 20, transcendentals=200_000),
        name="tables",
    )()


def over(value, divisor):
    return (value * (65536 // divisor + 1)) >> 16


def pack_kernel(amp_at, tilt_at, owner_at, row_at, col_at, out_at, *scratch):
    amp_ref, tilt_ref, owner_ref, row_ref, col_ref, out_ref, sems, out_sems = scratch
    copies = [
        pltpu.make_async_copy(place, ref, sems.at[k])
        for k, (place, ref) in enumerate(
            (
                (owner_at, owner_ref),
                (row_at, row_ref),
                (col_at, col_ref),
                (tilt_at, tilt_ref),
                (amp_at, amp_ref),
            )
        )
    ]
    for copy in copies:
        copy.start()
    count = amp_ref.shape[0]
    total = out_ref.shape[0]
    sub, lane = iota((count, count), 0), iota((count, count), 1)
    at = iota((total, count), 0)
    chip = over(at, ROWS)
    slot = at - ROWS * chip
    wanted = 2 * CAP * chip + slot - CAP * REACH
    wanted = jnp.where(slot >= SLOTS, -1, wanted).astype(F32)
    old = iota((256, 256), 0)
    new = ((old >> 4) & 7) * 32 + (old >> 7) * 16 + (old & 15)
    order = jnp.where(iota((256, 256), 1) == new, 1.0, 0.0).astype(BF16)
    word = iota((16, 256), 1)
    word = word - WORDS * over(word, WORDS)
    repeat = jnp.where(word == iota((16, 256), 0), 1.0, 0.0).astype(BF16)
    for copy in copies:
        copy.wait()
    row, col = row_ref[...], col_ref[...]
    owner = owner_ref[...].astype(F32)

    def upright(vector):
        picked = jnp.where(sub == lane, vector.astype(F32), 0.0)
        return jnp.sum(picked, axis=1, keepdims=True)

    same = (upright(owner) == owner) & (sub < lane)
    rank = jnp.sum(jnp.where(same, 1.0, 0.0), axis=0, keepdims=True)
    key = CAP * owner + rank
    chosen = jnp.where(wanted == key, 1.0, 0.0).astype(BF16)
    amp = amp_ref[...]
    turn_v = upright(col & 15).astype(jnp.int32)
    turn_u = upright(row & 15).astype(jnp.int32)
    within = iota(amp.shape, 1) & 15
    for step in (1, 2, 4, 8):
        moved = jnp.where(
            within >= step, pltpu.roll(amp, step, 1), pltpu.roll(amp, 240 + step, 1)
        )
        amp = jnp.where((turn_v & step) != 0, moved, amp)
    for step in (1, 2, 4, 8):
        amp = jnp.where((turn_u & step) != 0, pltpu.roll(amp, 16 * step, 1), amp)
    amp = mm(amp.astype(BF16), order).astype(BF16)
    tilt = tilt_ref[...]
    high = tilt.astype(BF16).astype(F32)
    middle = (tilt - high).astype(BF16).astype(F32)
    low = tilt - high - middle
    lines = [part[k : k + 1] for part in (high, middle, low) for k in range(3)]
    lines += [(row >> 4).astype(F32), (row & 15).astype(F32), col.astype(F32)]
    entry = iota((16, count), 0)
    extras = jnp.zeros((16, count), F32)
    for k, line in enumerate(lines):
        extras = jnp.where(entry == k, line, extras)
    extras = lax.dot_general(
        extras.astype(BF16), repeat, (((0,), (0,)), ((), ())), preferred_element_type=F32
    ).astype(BF16)
    both = jnp.concatenate([amp, extras], axis=1)
    part = total // PARTS
    line = iota((part, 256), 0)
    keep = over(iota((part, 256), 1), WORDS) == line - ROWS * over(line, ROWS)
    last = iota((part // ROWS, ROWS, 256), 1) == SLOTS
    sends = []
    for k in range(PARTS):
        rows = pl.ds(part * k, part)
        found = mm(chosen[part * k : part * k + part], both)
        placed = found[:, :256].reshape(part // ROWS, ROWS, 256)
        mine = jnp.where(keep, found[:, 256:], 0.0).reshape(part // ROWS, ROWS, 256)
        mine = jnp.sum(mine, axis=1, keepdims=True)
        out_ref[rows, :] = jnp.where(last, mine, placed).reshape(part, 256).astype(BF16)
        send = pltpu.make_async_copy(out_ref.at[rows], out_at.at[rows], out_sems.at[k])
        send.start()
        sends.append(send)
    for send in sends:
        send.wait()


def pack(amplitude, tilt, owner, row_offset, col_offset, chip_count):
    count = amplitude.shape[0]
    return pl.pallas_call(
        pack_kernel,
        out_shape=jax.ShapeDtypeStruct((chip_count * ROWS, 256), BF16),
        in_specs=[pl.BlockSpec(memory_space=pl.ANY)] * 5,
        out_specs=pl.BlockSpec(memory_space=pl.ANY),
        scratch_shapes=[
            pltpu.VMEM((count, 256), F32),
            pltpu.VMEM((3, count), F32),
            pltpu.VMEM((1, count), jnp.int32),
            pltpu.VMEM((1, count), jnp.int32),
            pltpu.VMEM((1, count), jnp.int32),
            pltpu.VMEM((chip_count * ROWS, 256), BF16),
            pltpu.SemaphoreType.DMA((5,)),
            pltpu.SemaphoreType.DMA((PARTS,)),
        ],
        compiler_params=pltpu.CompilerParams(vmem_limit_bytes=63 << 20),
        name="pack",
    )(
        amplitude,
        tilt,
        owner.reshape(1, count),
        row_offset.reshape(1, count),
        col_offset.reshape(1, count),
    )


def power_of(base_r, base_i, exponent, start_r, start_i):
    real, imag = start_r, start_i
    for bit in (1, 2, 4, 8):
        step = (exponent & bit) != 0
        turned_r = real * base_r - imag * base_i
        turned_i = real * base_i + imag * base_r
        real = jnp.where(step, turned_r, real)
        imag = jnp.where(step, turned_i, imag)
        base_r, base_i = base_r * base_r - base_i * base_i, 2.0 * base_r * base_i
    return real, imag


def row_transform(value, grow_ref, out_ref):
    product = mm(value, grow_ref[...])
    out_ref[0] = ((product[:TW, :HALF] - product[TW:, HALF:]) * SCALE).astype(BF16)
    out_ref[1] = ((product[:TW, HALF:] + product[TW:, :HALF]) * SCALE).astype(BF16)


class Arrivals:
    def __init__(self, inc_ref, facets_lo, facets_hi, param):
        self.sources = inc_ref.shape[0] // ROWS
        self.refs = facets_lo, facets_hi, param
        facets_lo[...] = inc_ref[:, :128].astype(F32)
        facets_hi[...] = inc_ref[:, 128:].astype(F32)
        pick = pl.ds(SLOTS, self.sources, stride=ROWS)
        extras = jnp.concatenate([facets_lo[pick, :], facets_hi[pick, :]], axis=1)
        entry = iota(extras.shape, 1)
        entry = entry - WORDS * over(entry, WORDS)
        tilt = extras + pltpu.roll(extras, 253, 1) + pltpu.roll(extras, 250, 1)
        tilt = jnp.where(entry < 3, tilt, pltpu.roll(tilt, 3, 1))
        turn_r, turn_i = cis(tilt)
        param[...] = jnp.where(entry < 3, turn_r, jnp.where(entry < 6, turn_i, extras))

    def slot(self, i):
        facets_lo, facets_hi, param = self.refs
        lanes = 8 * self.sources
        member = iota((8, lanes), 1) // self.sources
        residue = 8 * iota((8, lanes), 0) + member
        aside = iota((self.sources, 128), 1) < 32
        pick = pl.ds(i, self.sources, stride=ROWS)
        mine = pltpu.roll(param[...], (288 - WORDS * i) & 255, 1)[:, :128]
        blocks = []
        for half in (facets_lo[pick, :], facets_hi[pick, :]):
            blocks += [half] + [pltpu.roll(half, 128 - 32 * m, 1) for m in (1, 2, 3)]
        turned = jnp.concatenate([jnp.where(aside, block, mine) for block in blocks], axis=0).T
        par = turned[32:48]
        block, turn_u, col = [par[k : k + 1].astype(jnp.int32) for k in (9, 10, 11)]
        row_r, row_i = power_of(
            par[0:1], par[3:4], (residue - turn_u) & 15, par[2:3], par[5:6]
        )
        one = jnp.ones((16, lanes), F32)
        col_r, col_i = power_of(
            par[1:2], par[4:5], (iota((16, lanes), 0) - col) & 15, one, one * 0.0
        )
        spots = (block + jnp.where(residue < turn_u, 1, 0) + 32 * member).astype(F32)
        ahead = iota((TW, lanes), 0) - col
        window = jnp.where((ahead & -16) == 0, 1.0, 0.0).astype(BF16)
        return turned, row_r, row_i, col_r, col_i, spots, window


def column_kernel(mine_ref, beside_ref, lead_ref, out_ref, value_ref, *scratch):
    plane, total = scratch[-2:]
    arrivals = [Arrivals(mine_ref, *scratch[0:3]), Arrivals(beside_ref, *scratch[3:6])]
    fblk_ref, grow_ref = lead_ref.at[:TH], lead_ref.at[TH:]
    core = lax.axis_index("wide") & 1
    mx = iota((2 * TW, 1), 0) & (TW - 1)
    spot = iota((256, 8 * arrivals[0].sources), 0).astype(F32)
    for j in range(OFFSETS):
        slots = [part.slot(CAP * (core + j) + k) for part in arrivals for k in range(CAP)]
        for group in range(2):
            spreads, hots = [], []
            for turned, row_r, row_i, col_r, col_i, spots, window in slots:
                patch = turned[16 * group : 16 * group + 16]
                cos_p, sin_p = row_r[group : group + 1], row_i[group : group + 1]
                real = (patch * (cos_p * col_r - sin_p * col_i)).astype(BF16)
                imag = (patch * (cos_p * col_i + sin_p * col_r)).astype(BF16)
                spreads.append(
                    jnp.concatenate(
                        [jnp.concatenate([real] * 16, axis=0) * window]
                        + [jnp.concatenate([imag] * 16, axis=0) * window],
                        axis=0,
                    )
                )
                hots.append(
                    jnp.where(spot == spots[group : group + 1], 1.0, 0.0).astype(BF16)
                )
            spread = jnp.concatenate(spreads, axis=1)
            hot = jnp.concatenate(hots, axis=1)
            plane[j % 2, :, 256 * group : 256 * group + 256] = mm(spread, hot, NT).astype(BF16)
        weight = reach_weight(mx, TW, float(REACH - j))
        term = weight * mm(fblk_ref[...], plane[j % 2])
        total[...] = term if j == 0 else total[...] + term
    value = total[...].astype(BF16)
    value_ref[...] = value
    row_transform(value, grow_ref, out_ref)


def column_sums(mine, beside, lead):
    facets = [
        pltpu.VMEM((mine.shape[0], 128), F32),
        pltpu.VMEM((mine.shape[0], 128), F32),
        pltpu.VMEM((mine.shape[0] // ROWS, 256), F32),
    ]
    return pl.pallas_call(
        column_kernel,
        out_shape=(
            jax.ShapeDtypeStruct((2, TW, HALF), BF16),
            jax.ShapeDtypeStruct((2 * TW, TH), BF16),
        ),
        in_specs=[pl.BlockSpec(memory_space=pltpu.VMEM)] * 3,
        out_specs=tuple([pl.BlockSpec(memory_space=pltpu.VMEM)] * 2),
        scratch_shapes=facets
        + facets
        + [pltpu.VMEM((2, 2 * TW, TH), BF16), pltpu.VMEM((2 * TW, TH), F32)],
        compiler_params=pltpu.CompilerParams(vmem_limit_bytes=24 << 20),
        cost_estimate=pl.CostEstimate(flops=8_000_000_000, bytes_accessed=3 << 20, transcendentals=40_000),
        name="column_sums",
    )(mine, beside, lead)


def second_kernel(value_ref, grow_ref, out_ref):
    row_transform(value_ref[...], grow_ref, out_ref)


def second_half(value, grow):
    return pl.pallas_call(
        second_kernel,
        out_shape=jax.ShapeDtypeStruct((2, TW, HALF), BF16),
        in_specs=[pl.BlockSpec(memory_space=pltpu.VMEM)] * 2,
        out_specs=pl.BlockSpec(memory_space=pltpu.VMEM),
        compiler_params=pltpu.CompilerParams(vmem_limit_bytes=8 << 20),
        cost_estimate=pl.CostEstimate(flops=600_000_000, bytes_accessed=2 << 20, transcendentals=0),
        name="second_half",
    )(value, grow)


def image_kernel(half, *refs):
    side = (1 - 2 * (lax.axis_index("narrow") & 1)).astype(F32)
    pieces = refs[:OFFSETS]
    hblk_ref, kr_ref, ki_ref = refs[OFFSETS : OFFSETS + 3]
    my = iota((1, HALF), 1) + HALF * half
    weights = [reach_weight(my, TH, side * float(REACH - at)) for at in range(OFFSETS)]

    def band(part):
        acc = None
        for weight, piece in zip(weights, pieces):
            term = weight * piece[part].astype(F32)
            acc = term if acc is None else acc + term
        return acc.astype(BF16)

    image = mm(hblk_ref[...], jnp.concatenate([band(0), band(1)], axis=0)).astype(BF16)
    image_r, image_i = image[:TW], image[TW:]

    def share(rows, part):
        kr, ki = kr_ref[rows, :], ki_ref[rows, :]
        if part == 0:
            return (mm(kr, image_r, NT) - mm(ki, image_i, NT)) * SCALE
        return (mm(kr, image_i, NT) + mm(ki, image_r, NT)) * SCALE

    if half == 0:
        out_ref = refs[OFFSETS + 3]
        for part in range(2):
            out_ref[part] = share(pl.ds(0, TH), part)
        return
    before, out_at, out_ref, sems = refs[OFFSETS + 3 :]
    sends = []
    step = TH // 2
    for k in range(4):
        part, rows = k // 2, pl.ds(step * (k % 2), step)
        out_ref[part, rows, :] = share(rows, part) + before[part, rows, :]
        send = pltpu.make_async_copy(
            out_ref.at[part, rows], out_at.at[part, rows], sems.at[k]
        )
        send.start()
        sends.append(send)
    for send in sends:
        send.wait()


def image_of(half, pieces, tables, before):
    operands = (*pieces, *tables, *before)
    place = pl.ANY if half else pltpu.VMEM
    scratch = [pltpu.VMEM((2, TH, TW), F32), pltpu.SemaphoreType.DMA((4,))] if half else []
    return pl.pallas_call(
        functools.partial(image_kernel, half),
        out_shape=jax.ShapeDtypeStruct((2, TH, TW), F32),
        in_specs=[pl.BlockSpec(memory_space=pltpu.VMEM)] * len(operands),
        out_specs=pl.BlockSpec(memory_space=place),
        scratch_shapes=scratch,
        compiler_params=pltpu.CompilerParams(vmem_limit_bytes=16 << 20),
        cost_estimate=pl.CostEstimate(flops=900_000_000, bytes_accessed=4 << 20, transcendentals=0),
        name="image",
    )(*operands)


def swap(value, first):
    count = lax.axis_size("narrow")
    pairs = [(low, low + 1) for low in range(first, count - 1, 2)]
    return lax.ppermute(value, "narrow", pairs + [(high, low) for low, high in pairs])


def narrow_pieces(mine):
    above1 = swap(mine, 0)
    below1 = swap(mine, 1)
    above2 = swap(below1, 0)
    below2 = swap(above1, 1)
    return [below2, below1, mine, above1, above2]


def local(amplitude, tilt, owner, row_offset, col_offset):
    wide_count = lax.axis_size("wide")
    chip_count = wide_count // 2
    lead, grow_b, hblk, kr_a, ki_a, kr_b, ki_b = make_tables()
    outgoing = pack(amplitude, tilt, owner, row_offset, col_offset, chip_count)
    mine = lax.all_to_all(
        outgoing.reshape(chip_count, ROWS, 256),
        "wide",
        split_axis=0,
        concat_axis=0,
        tiled=True,
        axis_index_groups=[list(range(core, wide_count, 2)) for core in range(2)],
    ).reshape(chip_count * ROWS, 256)
    beside = lax.ppermute(mine, "wide", [(at, at ^ 1) for at in range(wide_count)])
    first, value = column_sums(mine, beside, lead)
    second = second_half(value, grow_b)
    partial = image_of(0, narrow_pieces(first), (hblk, kr_a, ki_a), ())
    return image_of(1, narrow_pieces(second), (hblk, kr_b, ki_b), (partial,))


def solution(mesh):
    in_specs = (
        P(("wide", "narrow"), None),
        P(None, ("wide", "narrow")),
        P(("wide", "narrow"), None),
        P(("wide", "narrow")),
        P(("wide", "narrow")),
    )
    out_specs = P(None, "narrow", "wide")
    return jax.shard_map(local, mesh=mesh, in_specs=in_specs, out_specs=out_specs, check_vma=False)
```

```python
import functools
import math

import jax
import jax.numpy as jnp
from jax import lax
from jax.experimental import pallas as pl
from jax.experimental.pallas import tpu as pltpu
from jax.sharding import PartitionSpec as P

TH = 512
TW = 256
FACET = 16
DEPTH = 1280
REACH = 2
OFFSETS = 2 * REACH + 1
CAP = 3
SLOTS = OFFSETS * CAP
HALF = TH // 2
PARTS = 4
ROWS = 16
SPREAD = 16.0
SCALE = 1.0 / math.sqrt(TH * TW)

F32 = jnp.float32
BF16 = jnp.bfloat16
NN = (((1,), (0,)), ((), ()))
NT = (((1,), (1,)), ((), ()))


def mm(a, b, dims=NN):
    return lax.dot_general(a, b, dims, preferred_element_type=F32)


def iota(shape, dim):
    return lax.broadcasted_iota(jnp.int32, shape, dim)


def cis(angle):
    return jnp.cos(angle), jnp.sin(angle)


def signed_frequency(position, length):
    return ((position + length // 2) & (length - 1)) - length // 2


def depth_phase(position, length):
    frequency = signed_frequency(position, length)
    turns = (DEPTH * frequency * frequency) & (2 * length * length - 1)
    return turns.astype(F32) * (-math.pi / (length * length))


def reach_weight(position, length, offset):
    travel = signed_frequency(position, length).astype(F32) * (DEPTH / (length * length))
    return jnp.exp(-((travel - offset) ** 2) / SPREAD)


def turn_angle(a, b, length):
    return ((a * b) & (length - 1)).astype(F32) * (2.0 * math.pi / length)


def table_kernel(lead_ref, grow_b_ref, hblk_ref, kr_a_ref, ki_a_ref, kr_b_ref, ki_b_ref):
    fblk_ref, grow_a_ref = lead_ref.at[:TH], lead_ref.at[TH:]
    fine_r, fine_i = cis(-turn_angle(iota((16, TW), 0), iota((16, TW), 1), TW))
    wide_r, wide_i = cis(-turn_angle(iota((16, TW), 0), iota((16, TW), 1), 16))
    for a in range(16):
        real = (wide_r[a : a + 1] * fine_r - wide_i[a : a + 1] * fine_i).astype(BF16)
        imag = (wide_r[a : a + 1] * fine_i + wide_i[a : a + 1] * fine_r).astype(BF16)
        at = 16 * a
        fblk_ref[at : at + 16, :TW] = real
        fblk_ref[at : at + 16, TW:] = -imag
        fblk_ref[TW + at : TW + at + 16, :TW] = imag
        fblk_ref[TW + at : TW + at + 16, TW:] = real
    wide_r, wide_i = cis(
        turn_angle(iota((16, TW), 0), iota((16, TW), 1), 16) + depth_phase(iota((16, TW), 1), TW)
    )
    for a in range(16):
        real = (wide_r[a : a + 1] * fine_r + wide_i[a : a + 1] * fine_i).astype(BF16)
        imag = (wide_i[a : a + 1] * fine_r - wide_r[a : a + 1] * fine_i).astype(BF16)
        at = 16 * a
        hblk_ref[at : at + 16, :TW] = real
        hblk_ref[at : at + 16, TW:] = -imag
        hblk_ref[TW + at : TW + at + 16, :TW] = imag
        hblk_ref[TW + at : TW + at + 16, TW:] = real
    fine_r, fine_i = cis(-turn_angle(iota((16, TH), 0), iota((16, TH), 1), TH))
    wide_r, wide_i = cis(-turn_angle(iota((32, TH), 0), iota((32, TH), 1), 32))
    for p in range(16):
        real = (fine_r[p : p + 1] * wide_r - fine_i[p : p + 1] * wide_i).astype(BF16)
        imag = (fine_r[p : p + 1] * wide_i + fine_i[p : p + 1] * wide_r).astype(BF16)
        at = 32 * p
        for k, ref in enumerate((grow_a_ref, grow_b_ref)):
            ref[at : at + 32, :HALF] = real[:, HALF * k : HALF * k + HALF]
            ref[at : at + 32, HALF:] = imag[:, HALF * k : HALF * k + HALF]
    wide_r, wide_i = cis(
        turn_angle(iota((32, TH), 0), iota((32, TH), 1), 32) + depth_phase(iota((32, TH), 1), TH)
    )
    for q in range(32):
        real = (wide_r[q : q + 1] * fine_r + wide_i[q : q + 1] * fine_i).astype(BF16)
        imag = (wide_i[q : q + 1] * fine_r - wide_r[q : q + 1] * fine_i).astype(BF16)
        at = 16 * q
        for k, (r_ref, i_ref) in enumerate(((kr_a_ref, ki_a_ref), (kr_b_ref, ki_b_ref))):
            r_ref[at : at + 16, :] = real[:, HALF * k : HALF * k + HALF]
            i_ref[at : at + 16, :] = imag[:, HALF * k : HALF * k + HALF]


def make_tables():
    square = jax.ShapeDtypeStruct((TH, TH), BF16)
    half = jax.ShapeDtypeStruct((TH, HALF), BF16)
    return pl.pallas_call(
        table_kernel,
        out_shape=(jax.ShapeDtypeStruct((2 * TH, TH), BF16), square, square, half, half, half, half),
        out_specs=tuple([pl.BlockSpec(memory_space=pltpu.VMEM)] * 7),
        compiler_params=pltpu.CompilerParams(vmem_limit_bytes=12 << 20),
        cost_estimate=pl.CostEstimate(flops=8_000_000, bytes_accessed=3 << 20, transcendentals=200_000),
        name="tables",
    )()


def pack_kernel(amp_at, tilt_at, owner_at, row_at, col_at, out_at, *scratch):
    amp_ref, tilt_ref, owner_ref, row_ref, col_ref, out_ref, sems, out_sems = scratch
    copies = [
        pltpu.make_async_copy(place, ref, sems.at[k])
        for k, (place, ref) in enumerate(
            (
                (owner_at, owner_ref),
                (row_at, row_ref),
                (col_at, col_ref),
                (tilt_at, tilt_ref),
                (amp_at, amp_ref),
            )
        )
    ]
    for copy in copies:
        copy.start()
    count = amp_ref.shape[0]
    total = out_ref.shape[0]
    sub, lane = iota((count, count), 0), iota((count, count), 1)
    at = iota((total, count), 0)
    wanted = CAP * (at >> 4) + (at & 15) - CAP * REACH
    wanted = jnp.where((at & 15) == SLOTS, -1, wanted).astype(F32)
    old = iota((256, 256), 0)
    new = ((old >> 4) & 3) * 64 + (old >> 6) * 16 + (old & 15)
    order = jnp.where(iota((256, 256), 1) == new, 1.0, 0.0).astype(BF16)
    repeat = jnp.where((iota((16, 256), 1) & 15) == iota((16, 256), 0), 1.0, 0.0).astype(BF16)
    for copy in copies:
        copy.wait()
    row, col = row_ref[...], col_ref[...]
    owner = owner_ref[...].astype(F32)

    def upright(vector):
        picked = jnp.where(sub == lane, vector.astype(F32), 0.0)
        return jnp.sum(picked, axis=1, keepdims=True)

    same = (upright(owner) == owner) & (sub < lane)
    rank = jnp.sum(jnp.where(same, 1.0, 0.0), axis=0, keepdims=True)
    key = CAP * owner + rank
    chosen = jnp.where(wanted == key, 1.0, 0.0).astype(BF16)
    amp = amp_ref[...]
    turn_v = upright(col & 15).astype(jnp.int32)
    turn_u = upright(row & 15).astype(jnp.int32)
    within = iota(amp.shape, 1) & 15
    for step in (1, 2, 4, 8):
        moved = jnp.where(
            within >= step, pltpu.roll(amp, step, 1), pltpu.roll(amp, 240 + step, 1)
        )
        amp = jnp.where((turn_v & step) != 0, moved, amp)
    for step in (1, 2, 4, 8):
        amp = jnp.where((turn_u & step) != 0, pltpu.roll(amp, 16 * step, 1), amp)
    amp = mm(amp.astype(BF16), order).astype(BF16)
    tilt = tilt_ref[...]
    high = tilt.astype(BF16).astype(F32)
    middle = (tilt - high).astype(BF16).astype(F32)
    low = tilt - high - middle
    lines = [part[k : k + 1] for part in (high, middle, low) for k in range(3)]
    lines += [(row >> 4).astype(F32), (row & 15).astype(F32), col.astype(F32)]
    entry = iota((16, count), 0)
    extras = jnp.zeros((16, count), F32)
    for k, line in enumerate(lines):
        extras = jnp.where(entry == k, line, extras)
    extras = lax.dot_general(
        extras.astype(BF16), repeat, (((0,), (0,)), ((), ())), preferred_element_type=F32
    ).astype(BF16)
    both = jnp.concatenate([amp, extras], axis=1)
    part = total // PARTS
    keep = (iota((part, 256), 1) >> 4) == (iota((part, 256), 0) & 15)
    last = iota((part // ROWS, ROWS, 256), 1) == SLOTS
    sends = []
    for k in range(PARTS):
        rows = pl.ds(part * k, part)
        found = mm(chosen[part * k : part * k + part], both)
        placed = found[:, :256].reshape(part // ROWS, ROWS, 256)
        mine = jnp.where(keep, found[:, 256:], 0.0).reshape(part // ROWS, ROWS, 256)
        mine = jnp.sum(mine, axis=1, keepdims=True)
        out_ref[rows, :] = jnp.where(last, mine, placed).reshape(part, 256).astype(BF16)
        send = pltpu.make_async_copy(out_ref.at[rows], out_at.at[rows], out_sems.at[k])
        send.start()
        sends.append(send)
    for send in sends:
        send.wait()


def pack(amplitude, tilt, owner, row_offset, col_offset, wide_count):
    count = amplitude.shape[0]
    return pl.pallas_call(
        pack_kernel,
        out_shape=jax.ShapeDtypeStruct((wide_count * ROWS, 256), BF16),
        in_specs=[pl.BlockSpec(memory_space=pl.ANY)] * 5,
        out_specs=pl.BlockSpec(memory_space=pl.ANY),
        scratch_shapes=[
            pltpu.VMEM((count, 256), F32),
            pltpu.VMEM((3, count), F32),
            pltpu.VMEM((1, count), jnp.int32),
            pltpu.VMEM((1, count), jnp.int32),
            pltpu.VMEM((1, count), jnp.int32),
            pltpu.VMEM((wide_count * ROWS, 256), BF16),
            pltpu.SemaphoreType.DMA((5,)),
            pltpu.SemaphoreType.DMA((PARTS,)),
        ],
        compiler_params=pltpu.CompilerParams(vmem_limit_bytes=63 << 20),
        name="pack",
    )(
        amplitude,
        tilt,
        owner.reshape(1, count),
        row_offset.reshape(1, count),
        col_offset.reshape(1, count),
    )


def power_of(base_r, base_i, exponent, start_r, start_i):
    real, imag = start_r, start_i
    for bit in (1, 2, 4, 8):
        step = (exponent & bit) != 0
        turned_r = real * base_r - imag * base_i
        turned_i = real * base_i + imag * base_r
        real = jnp.where(step, turned_r, real)
        imag = jnp.where(step, turned_i, imag)
        base_r, base_i = base_r * base_r - base_i * base_i, 2.0 * base_r * base_i
    return real, imag


def row_transform(value, grow_ref, out_ref):
    product = mm(value, grow_ref[...])
    out_ref[0] = ((product[:TW, :HALF] - product[TW:, HALF:]) * SCALE).astype(BF16)
    out_ref[1] = ((product[:TW, HALF:] + product[TW:, :HALF]) * SCALE).astype(BF16)


def column_kernel(inc_ref, lead_ref, out_ref, value_ref, facets_lo, facets_hi, param, plane, total):
    fblk_ref, grow_ref = lead_ref.at[:TH], lead_ref.at[TH:]
    sources = inc_ref.shape[0] // ROWS
    lanes = 4 * sources
    facets_lo[...] = inc_ref[:, :128].astype(F32)
    facets_hi[...] = inc_ref[:, 128:].astype(F32)
    total[...] = jnp.zeros_like(total)
    pick = pl.ds(SLOTS, sources, stride=ROWS)
    extras = jnp.concatenate([facets_lo[pick, :], facets_hi[pick, :]], axis=1)
    entry = iota(extras.shape, 1) & 15
    tilt = extras + pltpu.roll(extras, 253, 1) + pltpu.roll(extras, 250, 1)
    tilt = jnp.where(entry < 3, tilt, pltpu.roll(tilt, 3, 1))
    turn_r, turn_i = cis(tilt)
    param[...] = jnp.where(entry < 3, turn_r, jnp.where(entry < 6, turn_i, extras))
    mx = iota((2 * TW, 1), 0) & (TW - 1)
    member = iota((8, lanes), 1) // sources
    residue = 4 * iota((8, lanes), 0) + member
    spot = iota((128, lanes), 0).astype(F32)
    aside = iota((sources, 128), 1) < 64

    def one_slot(i):
        pick = pl.ds(i, sources, stride=ROWS)
        low, high = facets_lo[pick, :], facets_hi[pick, :]
        mine = pltpu.roll(param[...], (320 - 16 * i) & 255, 1)[:, :128]
        blocks = [low, pltpu.roll(low, 64, 1), high, pltpu.roll(high, 64, 1)]
        turned = jnp.concatenate([jnp.where(aside, block, mine) for block in blocks], axis=0).T
        par = turned[64:80]
        block, turn_u, col = [par[k : k + 1].astype(jnp.int32) for k in (9, 10, 11)]
        row_r, row_i = power_of(
            par[0:1], par[3:4], (residue - turn_u) & 15, par[2:3], par[5:6]
        )
        one = jnp.ones((16, lanes), F32)
        col_r, col_i = power_of(
            par[1:2], par[4:5], (iota((16, lanes), 0) - col) & 15, one, one * 0.0
        )
        spots = (block + jnp.where(residue < turn_u, 1, 0) + 32 * member).astype(F32)
        ahead = iota((TW, lanes), 0) - col
        window = jnp.where((ahead & -16) == 0, 1.0, 0.0).astype(BF16)
        return turned, row_r, row_i, col_r, col_i, spots, window

    def one_column(j, carry):
        slots = [one_slot(CAP * j + k) for k in range(CAP)]
        for group in range(4):
            spreads, hots = [], []
            for turned, row_r, row_i, col_r, col_i, spots, window in slots:
                patch = turned[16 * group : 16 * group + 16]
                cos_p, sin_p = row_r[group : group + 1], row_i[group : group + 1]
                real = (patch * (cos_p * col_r - sin_p * col_i)).astype(BF16)
                imag = (patch * (cos_p * col_i + sin_p * col_r)).astype(BF16)
                spreads.append(
                    jnp.concatenate(
                        [jnp.concatenate([real] * 16, axis=0) * window]
                        + [jnp.concatenate([imag] * 16, axis=0) * window],
                        axis=0,
                    )
                )
                hots.append(
                    jnp.where(spot == spots[group : group + 1], 1.0, 0.0).astype(BF16)
                )
            spread = jnp.concatenate(spreads, axis=1)
            hot = jnp.concatenate(hots, axis=1)
            plane[:, 128 * group : 128 * group + 128] = mm(spread, hot, NT).astype(BF16)
        weight = reach_weight(mx, TW, float(REACH - j))
        total[...] += weight * mm(fblk_ref[...], plane[...])
        return carry

    for j in range(OFFSETS):
        one_column(j, 0)
    value = total[...].astype(BF16)
    value_ref[...] = value
    row_transform(value, grow_ref, out_ref)


def column_sums(incoming, lead):
    return pl.pallas_call(
        column_kernel,
        out_shape=(
            jax.ShapeDtypeStruct((2, TW, HALF), BF16),
            jax.ShapeDtypeStruct((2 * TW, TH), BF16),
        ),
        in_specs=[pl.BlockSpec(memory_space=pltpu.VMEM)] * 2,
        out_specs=tuple([pl.BlockSpec(memory_space=pltpu.VMEM)] * 2),
        scratch_shapes=[
            pltpu.VMEM((incoming.shape[0], 128), F32),
            pltpu.VMEM((incoming.shape[0], 128), F32),
            pltpu.VMEM((incoming.shape[0] // ROWS, 256), F32),
            pltpu.VMEM((2 * TW, TH), BF16),
            pltpu.VMEM((2 * TW, TH), F32),
        ],
        compiler_params=pltpu.CompilerParams(vmem_limit_bytes=20 << 20),
        cost_estimate=pl.CostEstimate(flops=6_000_000_000, bytes_accessed=3 << 20, transcendentals=40_000),
        name="column_sums",
    )(incoming, lead)


def second_kernel(value_ref, grow_ref, out_ref):
    row_transform(value_ref[...], grow_ref, out_ref)


def second_half(value, grow):
    return pl.pallas_call(
        second_kernel,
        out_shape=jax.ShapeDtypeStruct((2, TW, HALF), BF16),
        in_specs=[pl.BlockSpec(memory_space=pltpu.VMEM)] * 2,
        out_specs=pl.BlockSpec(memory_space=pltpu.VMEM),
        compiler_params=pltpu.CompilerParams(vmem_limit_bytes=8 << 20),
        cost_estimate=pl.CostEstimate(flops=600_000_000, bytes_accessed=2 << 20, transcendentals=0),
        name="second_half",
    )(value, grow)


def image_kernel(half, *refs):
    side = (1 - 2 * (lax.axis_index("narrow") & 1)).astype(F32)
    pieces = refs[:OFFSETS]
    hblk_ref, kr_ref, ki_ref = refs[OFFSETS : OFFSETS + 3]
    my = iota((1, HALF), 1) + HALF * half
    weights = [reach_weight(my, TH, side * float(at - REACH)) for at in range(OFFSETS)]

    def band(part):
        acc = None
        for weight, piece in zip(weights, pieces):
            term = weight * piece[part].astype(F32)
            acc = term if acc is None else acc + term
        return acc.astype(BF16)

    image = mm(hblk_ref[...], jnp.concatenate([band(0), band(1)], axis=0)).astype(BF16)
    image_r, image_i = image[:TW], image[TW:]

    def share(rows, part):
        kr, ki = kr_ref[rows, :], ki_ref[rows, :]
        if part == 0:
            return (mm(kr, image_r, NT) - mm(ki, image_i, NT)) * SCALE
        return (mm(kr, image_i, NT) + mm(ki, image_r, NT)) * SCALE

    if half == 0:
        out_ref = refs[OFFSETS + 3]
        for part in range(2):
            out_ref[part] = share(pl.ds(0, TH), part)
        return
    before, out_at, out_ref, sems = refs[OFFSETS + 3 :]
    sends = []
    step = TH // 2
    for k in range(4):
        part, rows = k // 2, pl.ds(step * (k % 2), step)
        out_ref[part, rows, :] = share(rows, part) + before[part, rows, :]
        send = pltpu.make_async_copy(
            out_ref.at[part, rows], out_at.at[part, rows], sems.at[k]
        )
        send.start()
        sends.append(send)
    for send in sends:
        send.wait()


def image_of(half, pieces, tables, before):
    operands = (*pieces, *tables, *before)
    place = pl.ANY if half else pltpu.VMEM
    scratch = [pltpu.VMEM((2, TH, TW), F32), pltpu.SemaphoreType.DMA((4,))] if half else []
    return pl.pallas_call(
        functools.partial(image_kernel, half),
        out_shape=jax.ShapeDtypeStruct((2, TH, TW), F32),
        in_specs=[pl.BlockSpec(memory_space=pltpu.VMEM)] * len(operands),
        out_specs=pl.BlockSpec(memory_space=place),
        scratch_shapes=scratch,
        compiler_params=pltpu.CompilerParams(vmem_limit_bytes=16 << 20),
        cost_estimate=pl.CostEstimate(flops=900_000_000, bytes_accessed=4 << 20, transcendentals=0),
        name="image",
    )(*operands)


def swap(value, first):
    count = lax.axis_size("narrow")
    pairs = [(low, low + 1) for low in range(first, count - 1, 2)]
    return lax.ppermute(value, "narrow", pairs + [(high, low) for low, high in pairs])


def narrow_pieces(mine):
    below1 = swap(mine, 1)
    above1 = swap(mine, 0)
    above2 = swap(below1, 0)
    below2 = swap(above1, 1)
    return [above2, above1, mine, below1, below2]


def local(amplitude, tilt, owner, row_offset, col_offset):
    wide_count = lax.axis_size("wide")
    lead, grow_b, hblk, kr_a, ki_a, kr_b, ki_b = make_tables()
    outgoing = pack(amplitude, tilt, owner, row_offset, col_offset, wide_count)
    incoming = lax.all_to_all(
        outgoing.reshape(wide_count, ROWS, 256), "wide", split_axis=0, concat_axis=0, tiled=True
    ).reshape(wide_count * ROWS, 256)
    first, value = column_sums(incoming, lead)
    second = second_half(value, grow_b)
    partial = image_of(0, narrow_pieces(first), (hblk, kr_a, ki_a), ())
    return image_of(1, narrow_pieces(second), (hblk, kr_b, ki_b), (partial,))


def solution(mesh):
    in_specs = (
        P(("wide", "narrow"), None),
        P(None, ("wide", "narrow")),
        P(("wide", "narrow"), None),
        P(("wide", "narrow")),
        P(("wide", "narrow")),
    )
    out_specs = P(None, "narrow", "wide")
    return jax.shard_map(local, mesh=mesh, in_specs=in_specs, out_specs=out_specs, check_vma=False)
```

```python
import functools
import math

import jax
import jax.numpy as jnp
from jax import lax
from jax.experimental import pallas as pl
from jax.experimental.pallas import tpu as pltpu
from jax.sharding import PartitionSpec as P

TH = 512
TW = 256
FACET = 16
DEPTH = 1280
REACH = 2
OFFSETS = 2 * REACH + 1
CAP = 3
SLOTS = OFFSETS * CAP
HALF = TH // 2
PARTS = 4
ROWS = 16
SPREAD = 16.0
SCALE = 1.0 / math.sqrt(TH * TW)

F32 = jnp.float32
BF16 = jnp.bfloat16
NN = (((1,), (0,)), ((), ()))
NT = (((1,), (1,)), ((), ()))


def mm(a, b, dims=NN):
    return lax.dot_general(a, b, dims, preferred_element_type=F32)


def iota(shape, dim):
    return lax.broadcasted_iota(jnp.int32, shape, dim)


def cis(angle):
    return jnp.cos(angle), jnp.sin(angle)


def signed_frequency(position, length):
    return ((position + length // 2) & (length - 1)) - length // 2


def depth_phase(position, length):
    frequency = signed_frequency(position, length)
    turns = (DEPTH * frequency * frequency) & (2 * length * length - 1)
    return turns.astype(F32) * (-math.pi / (length * length))


def reach_weight(position, length, offset):
    travel = signed_frequency(position, length).astype(F32) * (DEPTH / (length * length))
    return jnp.exp(-((travel - offset) ** 2) / SPREAD)


def turn_angle(a, b, length):
    return ((a * b) & (length - 1)).astype(F32) * (2.0 * math.pi / length)


def table_kernel(lead_ref, grow_b_ref, hblk_ref, kr_a_ref, ki_a_ref, kr_b_ref, ki_b_ref):
    fblk_ref, grow_a_ref = lead_ref.at[:TH], lead_ref.at[TH:]
    fine_r, fine_i = cis(-turn_angle(iota((16, TW), 0), iota((16, TW), 1), TW))
    wide_r, wide_i = cis(-turn_angle(iota((16, TW), 0), iota((16, TW), 1), 16))
    for a in range(16):
        real = (wide_r[a : a + 1] * fine_r - wide_i[a : a + 1] * fine_i).astype(BF16)
        imag = (wide_r[a : a + 1] * fine_i + wide_i[a : a + 1] * fine_r).astype(BF16)
        at = 16 * a
        fblk_ref[at : at + 16, :TW] = real
        fblk_ref[at : at + 16, TW:] = -imag
        fblk_ref[TW + at : TW + at + 16, :TW] = imag
        fblk_ref[TW + at : TW + at + 16, TW:] = real
    wide_r, wide_i = cis(
        turn_angle(iota((16, TW), 0), iota((16, TW), 1), 16) + depth_phase(iota((16, TW), 1), TW)
    )
    for a in range(16):
        real = (wide_r[a : a + 1] * fine_r + wide_i[a : a + 1] * fine_i).astype(BF16)
        imag = (wide_i[a : a + 1] * fine_r - wide_r[a : a + 1] * fine_i).astype(BF16)
        at = 16 * a
        hblk_ref[at : at + 16, :TW] = real
        hblk_ref[at : at + 16, TW:] = -imag
        hblk_ref[TW + at : TW + at + 16, :TW] = imag
        hblk_ref[TW + at : TW + at + 16, TW:] = real
    fine_r, fine_i = cis(-turn_angle(iota((16, TH), 0), iota((16, TH), 1), TH))
    wide_r, wide_i = cis(-turn_angle(iota((32, TH), 0), iota((32, TH), 1), 32))
    for p in range(16):
        real = (fine_r[p : p + 1] * wide_r - fine_i[p : p + 1] * wide_i).astype(BF16)
        imag = (fine_r[p : p + 1] * wide_i + fine_i[p : p + 1] * wide_r).astype(BF16)
        at = 32 * p
        for k, ref in enumerate((grow_a_ref, grow_b_ref)):
            ref[at : at + 32, :HALF] = real[:, HALF * k : HALF * k + HALF]
            ref[at : at + 32, HALF:] = imag[:, HALF * k : HALF * k + HALF]
    wide_r, wide_i = cis(
        turn_angle(iota((32, TH), 0), iota((32, TH), 1), 32) + depth_phase(iota((32, TH), 1), TH)
    )
    for q in range(32):
        real = (wide_r[q : q + 1] * fine_r + wide_i[q : q + 1] * fine_i).astype(BF16)
        imag = (wide_i[q : q + 1] * fine_r - wide_r[q : q + 1] * fine_i).astype(BF16)
        at = 16 * q
        for k, (r_ref, i_ref) in enumerate(((kr_a_ref, ki_a_ref), (kr_b_ref, ki_b_ref))):
            r_ref[at : at + 16, :] = real[:, HALF * k : HALF * k + HALF]
            i_ref[at : at + 16, :] = imag[:, HALF * k : HALF * k + HALF]


def make_tables():
    square = jax.ShapeDtypeStruct((TH, TH), BF16)
    half = jax.ShapeDtypeStruct((TH, HALF), BF16)
    return pl.pallas_call(
        table_kernel,
        out_shape=(jax.ShapeDtypeStruct((2 * TH, TH), BF16), square, square, half, half, half, half),
        out_specs=tuple([pl.BlockSpec(memory_space=pltpu.VMEM)] * 7),
        compiler_params=pltpu.CompilerParams(vmem_limit_bytes=12 << 20),
        cost_estimate=pl.CostEstimate(flops=8_000_000, bytes_accessed=3 << 20, transcendentals=200_000),
        name="tables",
    )()


def pack_kernel(amp_at, tilt_at, owner_at, row_at, col_at, out_at, *scratch):
    amp_ref, tilt_ref, owner_ref, row_ref, col_ref, out_ref, sems, out_sems = scratch
    copies = [
        pltpu.make_async_copy(place, ref, sems.at[k])
        for k, (place, ref) in enumerate(
            (
                (owner_at, owner_ref),
                (row_at, row_ref),
                (col_at, col_ref),
                (tilt_at, tilt_ref),
                (amp_at, amp_ref),
            )
        )
    ]
    for copy in copies:
        copy.start()
    count = amp_ref.shape[0]
    total = out_ref.shape[0]
    sub, lane = iota((count, count), 0), iota((count, count), 1)
    at = iota((total, count), 0)
    wanted = CAP * (at >> 4) + (at & 15) - CAP * REACH
    wanted = jnp.where((at & 15) == SLOTS, -1, wanted).astype(F32)
    old = iota((256, 256), 0)
    new = ((old >> 4) & 3) * 64 + (old >> 6) * 16 + (old & 15)
    order = jnp.where(iota((256, 256), 1) == new, 1.0, 0.0).astype(BF16)
    repeat = jnp.where((iota((16, 256), 1) & 15) == iota((16, 256), 0), 1.0, 0.0).astype(BF16)
    for copy in copies:
        copy.wait()
    row, col = row_ref[...], col_ref[...]
    owner = owner_ref[...].astype(F32)

    def upright(vector):
        picked = jnp.where(sub == lane, vector.astype(F32), 0.0)
        return jnp.sum(picked, axis=1, keepdims=True)

    same = (upright(owner) == owner) & (sub < lane)
    rank = jnp.sum(jnp.where(same, 1.0, 0.0), axis=0, keepdims=True)
    key = CAP * owner + rank
    chosen = jnp.where(wanted == key, 1.0, 0.0).astype(BF16)
    amp = amp_ref[...]
    turn_v = upright(col & 15).astype(jnp.int32)
    turn_u = upright(row & 15).astype(jnp.int32)
    within = iota(amp.shape, 1) & 15
    for step in (1, 2, 4, 8):
        moved = jnp.where(
            within >= step, pltpu.roll(amp, step, 1), pltpu.roll(amp, 240 + step, 1)
        )
        amp = jnp.where((turn_v & step) != 0, moved, amp)
    for step in (1, 2, 4, 8):
        amp = jnp.where((turn_u & step) != 0, pltpu.roll(amp, 16 * step, 1), amp)
    amp = mm(amp.astype(BF16), order).astype(BF16)
    tilt = tilt_ref[...]
    high = tilt.astype(BF16).astype(F32)
    middle = (tilt - high).astype(BF16).astype(F32)
    low = tilt - high - middle
    lines = [part[k : k + 1] for part in (high, middle, low) for k in range(3)]
    lines += [(row >> 4).astype(F32), (row & 15).astype(F32), col.astype(F32)]
    entry = iota((16, count), 0)
    extras = jnp.zeros((16, count), F32)
    for k, line in enumerate(lines):
        extras = jnp.where(entry == k, line, extras)
    extras = lax.dot_general(
        extras.astype(BF16), repeat, (((0,), (0,)), ((), ())), preferred_element_type=F32
    ).astype(BF16)
    both = jnp.concatenate([amp, extras], axis=1)
    part = total // PARTS
    keep = (iota((part, 256), 1) >> 4) == (iota((part, 256), 0) & 15)
    last = iota((part // ROWS, ROWS, 256), 1) == SLOTS
    sends = []
    for k in range(PARTS):
        rows = pl.ds(part * k, part)
        found = mm(chosen[part * k : part * k + part], both)
        placed = found[:, :256].reshape(part // ROWS, ROWS, 256)
        mine = jnp.where(keep, found[:, 256:], 0.0).reshape(part // ROWS, ROWS, 256)
        mine = jnp.sum(mine, axis=1, keepdims=True)
        out_ref[rows, :] = jnp.where(last, mine, placed).reshape(part, 256).astype(BF16)
        send = pltpu.make_async_copy(out_ref.at[rows], out_at.at[rows], out_sems.at[k])
        send.start()
        sends.append(send)
    for send in sends:
        send.wait()


def pack(amplitude, tilt, owner, row_offset, col_offset, wide_count):
    count = amplitude.shape[0]
    return pl.pallas_call(
        pack_kernel,
        out_shape=jax.ShapeDtypeStruct((wide_count * ROWS, 256), BF16),
        in_specs=[pl.BlockSpec(memory_space=pl.ANY)] * 5,
        out_specs=pl.BlockSpec(memory_space=pl.ANY),
        scratch_shapes=[
            pltpu.VMEM((count, 256), F32),
            pltpu.VMEM((3, count), F32),
            pltpu.VMEM((1, count), jnp.int32),
            pltpu.VMEM((1, count), jnp.int32),
            pltpu.VMEM((1, count), jnp.int32),
            pltpu.VMEM((wide_count * ROWS, 256), BF16),
            pltpu.SemaphoreType.DMA((5,)),
            pltpu.SemaphoreType.DMA((PARTS,)),
        ],
        compiler_params=pltpu.CompilerParams(vmem_limit_bytes=63 << 20),
        name="pack",
    )(
        amplitude,
        tilt,
        owner.reshape(1, count),
        row_offset.reshape(1, count),
        col_offset.reshape(1, count),
    )


def power_of(base_r, base_i, exponent, start_r, start_i):
    real, imag = start_r, start_i
    for bit in (1, 2, 4, 8):
        step = (exponent & bit) != 0
        turned_r = real * base_r - imag * base_i
        turned_i = real * base_i + imag * base_r
        real = jnp.where(step, turned_r, real)
        imag = jnp.where(step, turned_i, imag)
        base_r, base_i = base_r * base_r - base_i * base_i, 2.0 * base_r * base_i
    return real, imag


def row_transform(value, grow_ref, out_ref):
    product = mm(value, grow_ref[...])
    out_ref[0] = ((product[:TW, :HALF] - product[TW:, HALF:]) * SCALE).astype(BF16)
    out_ref[1] = ((product[:TW, HALF:] + product[TW:, :HALF]) * SCALE).astype(BF16)


def column_kernel(inc_ref, lead_ref, out_ref, value_ref, facets_lo, facets_hi, param, plane, total):
    fblk_ref, grow_ref = lead_ref.at[:TH], lead_ref.at[TH:]
    sources = inc_ref.shape[0] // ROWS
    lanes = 4 * sources
    facets_lo[...] = inc_ref[:, :128].astype(F32)
    facets_hi[...] = inc_ref[:, 128:].astype(F32)
    total[...] = jnp.zeros_like(total)
    pick = pl.ds(SLOTS, sources, stride=ROWS)
    extras = jnp.concatenate([facets_lo[pick, :], facets_hi[pick, :]], axis=1)
    entry = iota(extras.shape, 1) & 15
    tilt = extras + pltpu.roll(extras, 253, 1) + pltpu.roll(extras, 250, 1)
    tilt = jnp.where(entry < 3, tilt, pltpu.roll(tilt, 3, 1))
    turn_r, turn_i = cis(tilt)
    param[...] = jnp.where(entry < 3, turn_r, jnp.where(entry < 6, turn_i, extras))
    mx = iota((2 * TW, 1), 0) & (TW - 1)
    member = iota((8, lanes), 1) // sources
    residue = 4 * iota((8, lanes), 0) + member
    spot = iota((128, lanes), 0).astype(F32)
    aside = iota((sources, 128), 1) < 64

    def one_slot(i):
        pick = pl.ds(i, sources, stride=ROWS)
        low, high = facets_lo[pick, :], facets_hi[pick, :]
        mine = pltpu.roll(param[...], (320 - 16 * i) & 255, 1)[:, :128]
        blocks = [low, pltpu.roll(low, 64, 1), high, pltpu.roll(high, 64, 1)]
        turned = jnp.concatenate([jnp.where(aside, block, mine) for block in blocks], axis=0).T
        par = turned[64:80]
        block, turn_u, col = [par[k : k + 1].astype(jnp.int32) for k in (9, 10, 11)]
        row_r, row_i = power_of(
            par[0:1], par[3:4], (residue - turn_u) & 15, par[2:3], par[5:6]
        )
        one = jnp.ones((16, lanes), F32)
        col_r, col_i = power_of(
            par[1:2], par[4:5], (iota((16, lanes), 0) - col) & 15, one, one * 0.0
        )
        spots = (block + jnp.where(residue < turn_u, 1, 0) + 32 * member).astype(F32)
        ahead = iota((TW, lanes), 0) - col
        window = jnp.where((ahead & -16) == 0, 1.0, 0.0).astype(BF16)
        return turned, row_r, row_i, col_r, col_i, spots, window

    def one_column(j, carry):
        slots = [one_slot(CAP * j + k) for k in range(CAP)]
        for group in range(4):
            spreads, hots = [], []
            for turned, row_r, row_i, col_r, col_i, spots, window in slots:
                patch = turned[16 * group : 16 * group + 16]
                cos_p, sin_p = row_r[group : group + 1], row_i[group : group + 1]
                real = (patch * (cos_p * col_r - sin_p * col_i)).astype(BF16)
                imag = (patch * (cos_p * col_i + sin_p * col_r)).astype(BF16)
                spreads.append(
                    jnp.concatenate(
                        [jnp.concatenate([real] * 16, axis=0) * window]
                        + [jnp.concatenate([imag] * 16, axis=0) * window],
                        axis=0,
                    )
                )
                hots.append(
                    jnp.where(spot == spots[group : group + 1], 1.0, 0.0).astype(BF16)
                )
            spread = jnp.concatenate(spreads, axis=1)
            hot = jnp.concatenate(hots, axis=1)
            plane[:, 128 * group : 128 * group + 128] = mm(spread, hot, NT).astype(BF16)
        weight = reach_weight(mx, TW, float(REACH - j))
        total[...] += weight * mm(fblk_ref[...], plane[...])
        return carry

    for j in range(OFFSETS):
        one_column(j, 0)
    value = total[...].astype(BF16)
    value_ref[...] = value
    row_transform(value, grow_ref, out_ref)


def column_sums(incoming, lead):
    return pl.pallas_call(
        column_kernel,
        out_shape=(
            jax.ShapeDtypeStruct((2, TW, HALF), BF16),
            jax.ShapeDtypeStruct((2 * TW, TH), BF16),
        ),
        in_specs=[pl.BlockSpec(memory_space=pltpu.VMEM)] * 2,
        out_specs=tuple([pl.BlockSpec(memory_space=pltpu.VMEM)] * 2),
        scratch_shapes=[
            pltpu.VMEM((incoming.shape[0], 128), F32),
            pltpu.VMEM((incoming.shape[0], 128), F32),
            pltpu.VMEM((incoming.shape[0] // ROWS, 256), F32),
            pltpu.VMEM((2 * TW, TH), BF16),
            pltpu.VMEM((2 * TW, TH), F32),
        ],
        compiler_params=pltpu.CompilerParams(vmem_limit_bytes=20 << 20),
        cost_estimate=pl.CostEstimate(flops=6_000_000_000, bytes_accessed=3 << 20, transcendentals=40_000),
        name="column_sums",
    )(incoming, lead)


def second_kernel(value_ref, grow_ref, first_ref, out_ref, both_ref):
    row_transform(value_ref[...], grow_ref, out_ref)
    both_ref[0] = first_ref[...]
    both_ref[1] = out_ref[...]


def second_half(value, grow, first):
    return pl.pallas_call(
        second_kernel,
        out_shape=(
            jax.ShapeDtypeStruct((2, TW, HALF), BF16),
            jax.ShapeDtypeStruct((2, 2, TW, HALF), BF16),
        ),
        in_specs=[pl.BlockSpec(memory_space=pltpu.VMEM)] * 3,
        out_specs=tuple([pl.BlockSpec(memory_space=pltpu.VMEM)] * 2),
        compiler_params=pltpu.CompilerParams(vmem_limit_bytes=8 << 20),
        cost_estimate=pl.CostEstimate(flops=600_000_000, bytes_accessed=2 << 20, transcendentals=0),
        name="second_half",
    )(value, grow, first)


def image_kernel(half, *refs):
    side = (1 - 2 * (lax.axis_index("narrow") & 1)).astype(F32)
    pieces = [refs[0], refs[1], refs[2], refs[3].at[half], refs[4]]
    hblk_ref, kr_ref, ki_ref = refs[OFFSETS : OFFSETS + 3]
    my = iota((1, HALF), 1) + HALF * half
    weights = [reach_weight(my, TH, side * float(REACH - at)) for at in range(OFFSETS)]

    def band(part):
        acc = None
        for weight, piece in zip(weights, pieces):
            term = weight * piece[part].astype(F32)
            acc = term if acc is None else acc + term
        return acc.astype(BF16)

    image = mm(hblk_ref[...], jnp.concatenate([band(0), band(1)], axis=0)).astype(BF16)
    image_r, image_i = image[:TW], image[TW:]

    def share(rows, part):
        kr, ki = kr_ref[rows, :], ki_ref[rows, :]
        if part == 0:
            return (mm(kr, image_r, NT) - mm(ki, image_i, NT)) * SCALE
        return (mm(kr, image_i, NT) + mm(ki, image_r, NT)) * SCALE

    if half == 0:
        out_ref = refs[OFFSETS + 3]
        for part in range(2):
            out_ref[part] = share(pl.ds(0, TH), part)
        return
    before, out_at, out_ref, sems = refs[OFFSETS + 3 :]
    sends = []
    step = TH // 2
    for k in range(4):
        part, rows = k // 2, pl.ds(step * (k % 2), step)
        out_ref[part, rows, :] = share(rows, part) + before[part, rows, :]
        send = pltpu.make_async_copy(
            out_ref.at[part, rows], out_at.at[part, rows], sems.at[k]
        )
        send.start()
        sends.append(send)
    for send in sends:
        send.wait()


def image_of(half, pieces, tables, before):
    operands = (*pieces, *tables, *before)
    place = pl.ANY if half else pltpu.VMEM
    scratch = [pltpu.VMEM((2, TH, TW), F32), pltpu.SemaphoreType.DMA((4,))] if half else []
    return pl.pallas_call(
        functools.partial(image_kernel, half),
        out_shape=jax.ShapeDtypeStruct((2, TH, TW), F32),
        in_specs=[pl.BlockSpec(memory_space=pltpu.VMEM)] * len(operands),
        out_specs=pl.BlockSpec(memory_space=place),
        scratch_shapes=scratch,
        compiler_params=pltpu.CompilerParams(vmem_limit_bytes=16 << 20),
        cost_estimate=pl.CostEstimate(flops=900_000_000, bytes_accessed=4 << 20, transcendentals=0),
        name="image",
    )(*operands)


def swap(value, first):
    count = lax.axis_size("narrow")
    pairs = [(low, low + 1) for low in range(first, count - 1, 2)]
    return lax.ppermute(value, "narrow", pairs + [(high, low) for low, high in pairs])


def narrow_pieces(both, halves):
    above1 = swap(both, 0)
    pieces = []
    for half, mine in enumerate(halves):
        below1 = swap(mine, 1)
        above2 = swap(below1, 0)
        below2 = swap(above1[half], 1)
        pieces.append([below2, below1, mine, above1, above2])
    return pieces


def local(amplitude, tilt, owner, row_offset, col_offset):
    wide_count = lax.axis_size("wide")
    lead, grow_b, hblk, kr_a, ki_a, kr_b, ki_b = make_tables()
    outgoing = pack(amplitude, tilt, owner, row_offset, col_offset, wide_count)
    incoming = lax.all_to_all(
        outgoing.reshape(wide_count, ROWS, 256), "wide", split_axis=0, concat_axis=0, tiled=True
    ).reshape(wide_count * ROWS, 256)
    first, value = column_sums(incoming, lead)
    second, both = second_half(value, grow_b, first)
    pieces = narrow_pieces(both, (first, second))
    partial = image_of(0, pieces[0], (hblk, kr_a, ki_a), ())
    return image_of(1, pieces[1], (hblk, kr_b, ki_b), (partial,))


def solution(mesh):
    in_specs = (
        P(("wide", "narrow"), None),
        P(None, ("wide", "narrow")),
        P(("wide", "narrow"), None),
        P(("wide", "narrow")),
        P(("wide", "narrow")),
    )
    out_specs = P(None, "narrow", "wide")
    return jax.shard_map(local, mesh=mesh, in_specs=in_specs, out_specs=out_specs, check_vma=False)
```
